32 devices in a mesh: sec: 2 (over core), dp: 4 (over y, x), mp: 4 (over z).
Axes of the slice: x: 2, y: 2, z: 4, core: 2. Of those that a mesh axis runs over, the one named last changes fastest.
Arguments:
- section_rows: bfloat16 [2, 512, 4096], P('sec', 'dp'), may hold values from -6 to 6
- proj_weights: bfloat16 [2, 4096, 8, 128], P('sec', None, 'mp'), may hold values from -1 to 1
- out_grad: bfloat16 [512, 4096], P('dp'), may hold values from -6 to 6
- ffn_gain: float32 [4096], replicated, may hold values from 0.5 to 1.5
- ffn_in: bfloat16 [4096, 2, 1536], P(None, None, ('sec', 'mp')), may hold values from -0.09375 to 0.09375
- ffn_out: bfloat16 [1536, 4096], P(('sec', 'mp')), may hold values from -0.15625 to 0.15625
- grow_level: int32 [1536], P(('sec', 'mp')), may hold values from 0 to 4, as said below
- dec_seg: int32 [4, 128], P('dp'), may hold values from 0 to 1, never falling along the last dimension, each value on 1 to 96 neighbouring positions
- enc_seg: int32 [4, 128], P('dp'), may hold values from 0 to 1, never falling along the last dimension, each value on 1 to 96 neighbouring positions
Outputs:
- layer_out: bfloat16 [512, 4096], P('dp', ('sec', 'mp'))
- proj_grads: bfloat16 [2, 4096, 8, 128], P('sec', 'dp', 'mp')
The draws below stay inside these ranges and needn't reach their ends.
Inputs may be any that keep to these rules, and one draw needn't show every extreme that they name: `grow_level`: units below 1024 have level 4. `dec_seg`: each of the 2 examples has entries in every group. `enc_seg`: each of the 2 examples has entries in every group.
All inputs are finite; a program needn't handle non-finite values.
Results may differ from the reference program's by a relative error of at most 0.025.
Values may be sent and summed in bfloat16 or wider, within the bound.
A program may use at most 64 MiB of HBM per device.

```python
import math
import jax
import jax.numpy as jnp
import numpy as np
from jax import lax

D = 4096
DH = 64
ROWS_DEV = 128
EXAMPLES = 2
HEADS = 8
FFW = 1536
NEW_W = 512
ROWS = 512
SHARDS = 4
N_DP = 4


def draw_grow_level(key, part):
    unit_index = jnp.arange(FFW)
    fresh = jax.random.randint(key, (FFW,), 0, 5)
    return jnp.where(unit_index < FFW - NEW_W, 4, fresh).astype(jnp.int32)


def draw_section_rows(key, part):
    full_shape = (2, ROWS, D)
    return jnp.clip(jax.random.normal(key, full_shape, jnp.float32), -6.0, 6.0).astype(jnp.bfloat16)


def draw_proj_weights(key, part):
    full_shape = (2, D, HEADS, 2 * DH)
    random_part = jnp.clip(jax.random.normal(key, full_shape, jnp.float32), -4.0, 4.0)
    column_ids = jnp.arange(2 * DH)
    drawn_scale = 1.0 / math.sqrt(D)
    query_scale = 1.0 / math.sqrt(D * DH)
    second_scale = jnp.where(column_ids < DH, query_scale, drawn_scale)
    first_scale = jnp.full((2 * DH,), drawn_scale, jnp.float32)
    column_scale = jnp.stack([first_scale, second_scale])
    weights = random_part * column_scale[:, None, None, :]
    return weights.astype(jnp.bfloat16)


def block_levels(key, dims, cuts, smallest, largest):
    def one(position, parts):
        heights = jax.random.uniform(jax.random.fold_in(jax.random.fold_in(key, 6), position), (parts,), jnp.float32, smallest / len(cuts), largest / len(cuts))
        return jnp.repeat(jnp.exp(heights), dims[position] // parts).reshape((-1,) + (1,) * (len(dims) - position - 1))

    factor_of = one(*cuts[0])
    for cut in cuts[1:]:
        factor_of = factor_of * one(*cut)
    return factor_of


def split_up(number_of, total, most, slope):
    weights = [(1 << 20) // math.isqrt(rank ** slope) + 1 for rank in range(2, number_of + 1)]
    rest, given = total - most - (number_of - 1), [1] * (number_of - 1)
    while rest > 0:
        movable = [i for i in range(number_of - 1) if given[i] < most]
        whole, remaining = sum([weights[i] for i in movable]), rest
        for i in movable:
            addition = min(most - given[i], max(1, remaining * weights[i] // whole), rest)
            given[i] = given[i] + addition
            rest = rest - addition
    return np.array([most] + given)


def ragged(own_key, amount, total, bound, lean):
    if amount == 2:
        one = jax.random.randint(own_key, (), max(1, total - bound), min(bound, total - 1) + 1)
        return jnp.stack([one, total - one])
    sizes = jnp.asarray(split_up(amount, total, bound, lean), jnp.int32)
    twos = (amount - 1) // 2
    giver, sink = sizes[1:1 + 2 * twos:2], sizes[2:2 + 2 * twos:2]
    slack = jnp.minimum(giver - 1, bound - sink)
    passed = jax.random.randint(jax.random.fold_in(own_key, 1), (twos,), 0, 1 << 20) % (slack + 1)
    sizes = sizes.at[1:1 + 2 * twos:2].set(giver - passed).at[2:2 + 2 * twos:2].set(sink + passed)
    return sizes[jax.random.permutation(jax.random.fold_in(own_key, 2), amount)]


def centred(rng, dims, deviation, most, cuts=(), dtype=jnp.bfloat16):
    array = jax.random.normal(rng, dims, jnp.float32) * deviation
    if len(cuts) > 0:
        array = block_levels(rng, dims, cuts, -0.22, 0.18) * array
    return jnp.clip(array, min=-most, max=most).astype(dtype)


def setup_inputs(seed: int = 0) -> dict:
    keys = jax.random.split(jax.random.key(seed), 10)
    return {
        "section_rows": draw_section_rows(jax.random.fold_in(keys[9], 71), 0),
        "proj_weights": draw_proj_weights(jax.random.fold_in(keys[9], 71), 0),
        "out_grad": centred(keys[2], (ROWS, D), 1.0, 6.0, ((0, 4),)),
        "ffn_gain": jnp.clip(1.0 + 0.1 * jax.random.normal(keys[3], (D,), jnp.float32), 0.5, 1.5),
        "ffn_in": centred(keys[4], (D, 2, FFW), D ** -0.5, 0.09375, ((2, 8),)),
        "ffn_out": centred(keys[5], (FFW, D), FFW ** -0.5, 0.15625, ((0, 8),)),
        "grow_level": draw_grow_level(jax.random.fold_in(keys[9], 71), 0),
        "dec_seg": jax.vmap(lambda own: jnp.searchsorted(jnp.cumsum(ragged(own, EXAMPLES, ROWS_DEV, ROWS_DEV * 3 // 4, 2)), jnp.arange(ROWS_DEV), side="right"))(jax.random.split(keys[7], SHARDS)).reshape((SHARDS, ROWS_DEV)).astype(jnp.int32),
        "enc_seg": jax.vmap(lambda own: jnp.searchsorted(jnp.cumsum(ragged(own, EXAMPLES, ROWS_DEV, ROWS_DEV * 3 // 4, 2)), jnp.arange(ROWS_DEV), side="right"))(jax.random.split(keys[8], SHARDS)).reshape((SHARDS, ROWS_DEV)).astype(jnp.int32),
    }


norm_eps = 1e-06

def attend(queries, key_part, value_part, same_example):
    scores = jnp.einsum('bqhd,bkhd->bhqk', queries.astype(jnp.float32), key_part.astype(jnp.float32))
    scores = jnp.where(same_example[:, None], scores, -1e+30)
    scores = scores - lax.optimization_barrier(jnp.max(scores, axis=-1, keepdims=True))
    exponent = jnp.exp(scores)
    attn_prob = exponent / lax.optimization_barrier(jnp.sum(exponent, axis=-1, keepdims=True))
    prob_low = attn_prob.astype(jnp.bfloat16)
    context = jnp.einsum('bhqk,bkhd->bqhd', prob_low.astype(jnp.float32), value_part.astype(jnp.float32)).astype(jnp.bfloat16)
    return (attn_prob, prob_low, context)

def attend_back(queries, key_part, value_part, attn_prob, prob_low, grad_context):
    grad_prob = jnp.einsum('bqhe,bkhe->bhqk', grad_context.astype(jnp.float32), value_part.astype(jnp.float32))
    grad_score = (attn_prob * (grad_prob - lax.optimization_barrier(jnp.sum(grad_prob * attn_prob, axis=-1, keepdims=True)))).astype(jnp.bfloat16)
    score_f = grad_score.astype(jnp.float32)
    grad_query = jnp.einsum('bhqk,bkhd->bqhd', score_f, key_part.astype(jnp.float32)).astype(jnp.bfloat16)
    grad_key = jnp.einsum('bhqk,bqhd->bkhd', score_f, queries.astype(jnp.float32)).astype(jnp.bfloat16)
    grad_value = jnp.einsum('bhqk,bqhe->bkhe', prob_low.astype(jnp.float32), grad_context.astype(jnp.float32)).astype(jnp.bfloat16)
    return (grad_query, grad_key, grad_value)

def rounded(value):
    return lax.optimization_barrier(value.astype(jnp.bfloat16)).astype(jnp.float32)

def reference(section_rows, proj_weights, out_grad, ffn_gain, ffn_in, ffn_out, grow_level, dec_seg, enc_seg):
    enc_rows = section_rows[0]
    dec_rows = section_rows[1]
    kv_weight = proj_weights[0].astype(jnp.float32)
    qo_weight = proj_weights[1].astype(jnp.float32)
    key_value = jnp.einsum('rd,dhe->rhe', enc_rows.astype(jnp.float32), kv_weight).astype(jnp.bfloat16)
    query_full = jnp.einsum('rd,dhe->rhe', dec_rows.astype(jnp.float32), qo_weight[..., :DH]).astype(jnp.bfloat16)
    split_shape = (N_DP, ROWS_DEV, HEADS, DH)
    queries = query_full.reshape(split_shape)
    key_part = key_value[..., :DH].reshape(split_shape)
    value_part = key_value[..., DH:].reshape(split_shape)
    same_example = dec_seg[:, :, None] == enc_seg[:, None, :]
    attn_prob, prob_low, context = attend(queries, key_part, value_part, same_example)
    out_weight = qo_weight[..., DH:]
    context_rows = context.reshape(ROWS, HEADS, DH)
    attn_out = jnp.einsum('rhe,dhe->rd', context_rows.astype(jnp.float32), out_weight)
    mixed_rows = (dec_rows.astype(jnp.float32) + attn_out).astype(jnp.bfloat16)
    mixed_wide = mixed_rows.astype(jnp.float32)
    inverse = lax.rsqrt(lax.optimization_barrier(jnp.mean(mixed_wide * mixed_wide, axis=-1, keepdims=True)) + norm_eps)
    normed = (mixed_wide * inverse * ffn_gain).astype(jnp.bfloat16)
    gate_up = jnp.einsum('rd,dcf->rcf', normed.astype(jnp.float32), ffn_in.astype(jnp.float32))
    unit_level = grow_level.astype(jnp.float32) * 0.25
    hidden = (jax.nn.gelu(gate_up[:, 0], approximate=True) * gate_up[:, 1] * unit_level).astype(jnp.bfloat16)
    layer_out = (mixed_wide + jnp.dot(hidden, ffn_out, preferred_element_type=jnp.float32)).astype(jnp.bfloat16)
    grad_context = jnp.einsum('rd,dhe->rhe', out_grad.astype(jnp.float32), out_weight).astype(jnp.bfloat16).reshape(split_shape)
    grad_query, grad_key, grad_value = attend_back(queries, key_part, value_part, attn_prob, prob_low, grad_context)
    enc_groups = enc_rows.reshape(N_DP, ROWS_DEV, D)
    dec_groups = dec_rows.reshape(N_DP, ROWS_DEV, D)
    grad_groups = out_grad.reshape(N_DP, ROWS_DEV, D)

    def accumulate(carry, pieces):
        enc_piece, dec_piece, grad_piece, query_grad, key_grad, value_grad, context_piece = pieces
        enc_wide = enc_piece.astype(jnp.float32)
        key_side = jnp.concatenate([jnp.einsum('rd,rhe->dhe', enc_wide, key_grad.astype(jnp.float32)), jnp.einsum('rd,rhe->dhe', enc_wide, value_grad.astype(jnp.float32))], axis=-1)
        query_side = jnp.concatenate([jnp.einsum('rd,rhe->dhe', dec_piece.astype(jnp.float32), query_grad.astype(jnp.float32)), jnp.einsum('rd,rhe->dhe', grad_piece.astype(jnp.float32), context_piece.astype(jnp.float32))], axis=-1)
        return ((carry[0] + rounded(key_side), carry[1] + rounded(query_side)), None)
    empty = jnp.zeros((D, HEADS, 2 * DH), jnp.float32)
    totals, _ = lax.scan(accumulate, (empty, empty), (enc_groups, dec_groups, grad_groups, grad_query, grad_key, grad_value, context))
    proj_grads = jnp.stack([totals[0], totals[1]]).astype(jnp.bfloat16)
    return (layer_out, proj_grads)
```

```python
import functools
import math

import jax
import jax.numpy as jnp
from jax import lax
from jax.experimental import pallas as pl
from jax.experimental.pallas import tpu as pltpu
from jax.sharding import PartitionSpec as P

norm_eps = 1e-06
pieces = 2
most_relays = 4
F32 = jnp.float32
BF16 = jnp.bfloat16


def contract(left, right, left_dim, right_dim):
    dims = (((left_dim,), (right_dim,)), ((), ()))
    return lax.dot_general(left, right, dims, preferred_element_type=F32)


def remote(src, dst, send, recv, device):
    return pltpu.make_async_remote_copy(
        src_ref=src,
        dst_ref=dst,
        send_sem=send,
        recv_sem=recv,
        device_id=device,
        device_id_type=pl.DeviceIdType.MESH,
    )


def body(
    n_dp,
    n_mp,
    rows_hbm,
    weight_hbm,
    grad_hbm,
    gain_hbm,
    ffn_in_hbm,
    ffn_out_hbm,
    level_hbm,
    dec_seg_hbm,
    enc_seg_hbm,
    layer_out,
    proj_grads,
    rows,
    weight,
    grad,
    gain,
    ffn_in,
    level,
    dec_seg,
    enc_seg,
    down_own,
    down_other,
    w_left,
    w_right,
    kv_send,
    kv_recv,
    wo_all,
    ctx_all,
    rows_all,
    grad_all,
    g_send,
    g_all,
    mix,
    gate_up,
    square,
    hid_own,
    hid_other,
    partial,
    fold_send,
    fold_recv,
    t_left,
    t_right,
    rows_sem,
    grad_sem,
    g_sem,
    wo_sem,
    relay_sem,
    ctx_sem,
    mix_send,
    mix_recv,
    fwd_sem,
    hid_sem,
    fold_sem,
    fold_got,
    kv_sem,
    gkv_sem,
    down_sem,
    weight_sem,
    load_sem,
    slot_sem,
):
    sec = lax.axis_index("sec")
    dp = lax.axis_index("dp")
    mp = lax.axis_index("mp")
    n_rows, width = rows.shape
    lanes = weight.shape[1]
    half = lanes // 2
    block = width // n_mp
    share = width // (2 * n_mp)
    cut = width // n_dp
    units = down_own.shape[0]
    hubs = n_mp == 4
    if hubs:
        hub = mp * (3 - mp) // 2
        mate = mp + 1 - 2 * lax.rem(mp, 2)
        far_hub = 3 - mp * hub - mate * (1 - hub)
        far_end = 3 - mate * hub - mp * (1 - hub)
        arrivals = [mate, far_hub, far_end]
        targets = [mate, 2 - mp // 2]
        is_hub = hub == 1
    else:
        arrivals = [lax.rem(mp + n_mp - t, n_mp) for t in range(1, n_mp)]
        targets = [lax.rem(mp + t, n_mp) for t in range(1, n_mp)]
    piece_rows = n_rows // pieces
    relays = math.gcd(n_dp, most_relays)
    part = block // relays
    turn = lax.rem(dp, relays)
    is_dec = sec == 1
    is_enc = sec == 0
    other = {"sec": 1 - sec}

    def dp_at(t):
        return lax.rem(dp + t, n_dp)

    def mp_at(t):
        return lax.rem(mp + t, n_mp)

    def turn_at(s):
        return lax.rem(turn + s, relays)

    def cols(index, size):
        return pl.ds(pl.multiple_of(index * size, size), size)

    def piece(c):
        return pl.ds(c * piece_rows, piece_rows)

    def signal(device):
        pl.semaphore_signal(barrier, inc=1, device_id=device, device_id_type=pl.DeviceIdType.MESH)

    def weight_load(t):
        where = cols(mp_at(t), 2 * block)
        return pltpu.make_async_copy(
            weight_hbm.at[where, :], weight.at[where, :], weight_sem.at[t]
        )

    pairs = (
        (rows_hbm, rows),
        (grad_hbm, grad),
        (dec_seg_hbm, dec_seg),
        (enc_seg_hbm, enc_seg),
        (gain_hbm, gain),
        (level_hbm, level),
        (ffn_in_hbm, ffn_in),
        (ffn_out_hbm.at[:, cols(sec, width // 2)], down_own),
    )
    loads = [pltpu.make_async_copy(a, b, load_sem.at[i]) for i, (a, b) in enumerate(pairs)]
    own_rows = pltpu.make_async_copy(rows_hbm.at[:, cols(dp, cut)], rows_all.at[0], slot_sem.at[0])
    own_grad = pltpu.make_async_copy(grad_hbm.at[:, cols(dp, cut)], grad_all.at[0], slot_sem.at[1])

    def rows_copy(t):
        to = dp_at(t)
        return remote(
            rows_hbm.at[:, cols(to, cut)], rows_all.at[t], rows_sem.at[0, t], rows_sem.at[1, t], {"dp": to}
        )

    def grad_copy(t):
        to = dp_at(t)
        return remote(
            grad_hbm.at[:, cols(to, cut)], grad_all.at[t], grad_sem.at[0, t], grad_sem.at[1, t], {"dp": to}
        )

    def g_copy(t):
        return remote(
            g_all.at[0], g_all.at[t], g_sem.at[0, t], g_sem.at[1, t], {"dp": dp_at(t)}
        )

    def slot(t):
        return slice(t * lanes, (t + 1) * lanes)

    def adjacent(t, sending):
        if t == 1:
            return mp < n_mp - 1 if sending else mp > 0
        return mp > 0 if sending else mp < n_mp - 1

    def near_far(t, sending, near, far):
        if 1 < t < n_mp - 1:
            far()
        else:
            pl.when(adjacent(t, sending))(near)
            pl.when(jnp.logical_not(adjacent(t, sending)))(far)

    def wo_copy(t):
        to = mp_at(t)
        return remote(
            w_right.at[cols(to * relays + turn, part), :],
            wo_all.at[cols(turn, part), slot(t)],
            wo_sem.at[0, t],
            wo_sem.at[1, t],
            {"mp": to},
        )

    def wo_whole(t):
        to = mp_at(t)
        return remote(
            w_right.at[cols(to, block), :],
            wo_all.at[:, slot(t)],
            wo_sem.at[0, t],
            wo_sem.at[1, t],
            {"mp": to},
        )

    def relay_out(t, s):
        ref = wo_all.at[cols(turn, part), slot(t)]
        to = {"dp": dp - turn + turn_at(s)}
        return remote(ref, ref, relay_sem.at[0, t, s], relay_sem.at[1, t, s], to)

    def relay_in(t, s):
        ref = wo_all.at[cols(turn_at(relays - s), part), slot(t)]
        to = {"dp": dp - turn + turn_at(s)}
        return remote(ref, ref, relay_sem.at[0, t, s], relay_sem.at[1, t, s], to)

    def ctx_copy(t):
        return remote(
            ctx_all.at[:, slot(0)],
            ctx_all.at[:, slot(t)],
            ctx_sem.at[0, t],
            ctx_sem.at[1, t],
            {"mp": mp_at(t)},
        )

    def mix_copy(c, b, j):
        ref = mix.at[b, piece(c), :]
        return remote(ref, ref, mix_send.at[j, c, b], mix_recv.at[c, b], {"mp": targets[j]})

    def fwd_copy(c, b):
        ref = mix.at[b, piece(c), :]
        return remote(ref, ref, fwd_sem.at[0, c, b], fwd_sem.at[1, c, b], other)

    def hid_copy(c):
        return remote(
            hid_own.at[piece(c), :], hid_other.at[piece(c), :], hid_sem.at[0, c], hid_sem.at[1, c], other
        )

    def fold_copy(c, k):
        if hubs:
            into = 1 + (1 - hub) * k if k else 0
            to = hub * arrivals[k] + (1 - hub) * mate
        else:
            into, to = k, arrivals[k]
        return remote(
            fold_send.at[k, piece(c), :],
            fold_recv.at[into, piece(c), :],
            fold_sem.at[c, k],
            fold_got.at[c, into],
            {"mp": to},
        )

    def fold_in(c, k):
        return remote(
            fold_send.at[0, piece(c), :],
            fold_recv.at[k, piece(c), :],
            fold_sem.at[c, 0],
            fold_got.at[c, k],
            {"mp": arrivals[0]},
        )

    kv_copy = remote(kv_send, kv_recv, kv_sem.at[0], kv_sem.at[1], other)
    gkv_copy = remote(g_send, g_all.at[0], gkv_sem.at[0], gkv_sem.at[1], other)
    down_copy = remote(
        ffn_out_hbm.at[:, cols(1 - sec, width // 2)], down_other, down_sem.at[0], down_sem.at[1], other
    )

    with jax.named_scope("signals"):
        barrier = pltpu.get_barrier_semaphore()
        for t in list(range(1, n_mp)) + [0]:
            weight_load(t).start()
        for load in loads[:1]:
            load.start()
        signal(other)
        for t in range(1, n_dp):
            signal({"dp": dp_at(t)})
        for t in range(1, n_mp):
            signal({"mp": mp_at(t)})
        for load in loads[1:6]:
            load.start()

    tile = 2 * lanes
    out_id = lax.broadcasted_iota(jnp.int32, (tile, tile), 0)
    in_id = lax.broadcasted_iota(jnp.int32, (tile, tile), 1)
    wanted = jnp.where(out_id < lanes, 2 * out_id, 2 * (out_id - lanes) + 1)
    pick = jnp.where(in_id == wanted, 1.0, 0.0).astype(BF16)
    first = lax.broadcasted_iota(jnp.int32, (lanes, lanes), 1) < half

    with jax.named_scope("split"):
        for t in list(range(1, n_mp)) + [0]:
            begin = mp_at(t) * block
            weight_load(t).wait()
            for i in range(block // lanes):
                d = pl.multiple_of(begin + i * lanes, lanes)
                two = contract(pick, weight[pl.ds(pl.multiple_of(2 * d, tile), tile), :], 1, 0)
                one, second = two[:lanes], two[lanes:]
                w_left[pl.ds(d, lanes), :] = jnp.where(
                    first, one, pltpu.roll(second, half, 1)
                ).astype(BF16)
                w_right[pl.ds(d, lanes), :] = jnp.where(
                    first, pltpu.roll(one, half, 1), second
                ).astype(BF16)

    with jax.named_scope("barrier"):
        pl.semaphore_wait(barrier, n_dp + n_mp - 1)

    @pl.when(is_dec)
    def _():
        with jax.named_scope("wo_start"):
            for whole in range(2):
                for t in range(1, n_mp):
                    near_far(
                        t,
                        True,
                        (lambda: wo_whole(t).start()) if whole else (lambda: None),
                        (lambda: None) if whole else (lambda: wo_copy(t).start()),
                    )

    loads[0].wait()

    @pl.when(is_enc)
    def _():
        with jax.named_scope("kv"):
            kv_send[0] = contract(rows[...], w_left[...], 1, 0).astype(BF16)
            kv_send[1] = contract(rows[...], w_right[...], 1, 0).astype(BF16)
            kv_copy.start()
            rows_copy(1).start()

    for load in loads[6:]:
        load.start()
    own_rows.start()
    down_copy.start()
    for load in loads[1:6]:
        load.wait()

    @pl.when(is_dec)
    def _():
        own_grad.start()
        with jax.named_scope("q_gc"):
            wide_q = contract(rows[...], w_left[...], 1, 0)
            wide_gc = contract(grad[...], w_right[...], 1, 0)
            q = wide_q.astype(BF16)
            gc = wide_gc.astype(BF16)
            dec = jnp.transpose(jnp.broadcast_to(dec_seg[...].astype(F32), (n_rows, n_rows)))
            same = dec == jnp.broadcast_to(enc_seg[...].astype(F32), (n_rows, n_rows))
            wo_all[:, slot(0)] = w_right[cols(mp, block), :]
        with jax.named_scope("relay"):
            for t in range(1, n_mp):

                def pass_quarter():
                    wo_copy(t).wait_recv()
                    for s in range(1, relays):
                        relay_out(t, s).start()

                near_far(t, False, lambda: None, pass_quarter)
        with jax.named_scope("kv_wait"):
            kv_copy.wait_recv()
        with jax.named_scope("attend"):
            key = kv_recv[0]
            value = kv_recv[1]
            probs, lows, contexts = [], [], []
            for h in range(2):
                mine = first if h == 0 else jnp.logical_not(first)
                scores = contract(jnp.where(mine, wide_q, 0.0).astype(BF16), key, 1, 1)
                scores = jnp.where(same, scores, -1e30)
                scores = jnp.exp(scores - jnp.max(scores, axis=1, keepdims=True))
                prob = scores / jnp.sum(scores, axis=1, keepdims=True)
                low = prob.astype(BF16)
                probs.append(prob)
                lows.append(low)
                contexts.append(contract(low, value, 1, 0))
            context = jnp.where(first, contexts[0], contexts[1]).astype(BF16)
            ctx_all[:, slot(0)] = context
            g_all[0, :, lanes:] = context
            for t in range(1, n_mp):
                ctx_copy(t).start()
        with jax.named_scope("attend_back"):
            gqs, gks, gvs = [], [], []
            for h in range(2):
                mine = first if h == 0 else jnp.logical_not(first)
                grad_prob = contract(jnp.where(mine, wide_gc, 0.0).astype(BF16), value, 1, 1)
                total = jnp.sum(grad_prob * probs[h], axis=1, keepdims=True)
                score = (probs[h] * (grad_prob - total)).astype(BF16)
                gqs.append(contract(score, key, 1, 0))
                gks.append(contract(score, q, 0, 0))
                gvs.append(contract(lows[h], gc, 0, 0))
            g_send[:, :lanes] = jnp.where(first, gks[0], gks[1]).astype(BF16)
            g_send[:, lanes:] = jnp.where(first, gvs[0], gvs[1]).astype(BF16)
            gkv_copy.start()
            g_all[0, :, :lanes] = jnp.where(first, gqs[0], gqs[1]).astype(BF16)

    @pl.when(is_enc)
    def _():
        with jax.named_scope("gkv_wait"):
            gkv_copy.wait_recv()
            for t in range(2, n_dp):
                rows_copy(t).start()

    for t in range(1, n_dp):
        g_copy(t).start()

    @pl.when(is_dec)
    def _():
        with jax.named_scope("wo_wait"):
            for t in range(1, n_mp):

                def take_quarters():
                    for s in range(1, relays):
                        relay_in(t, s).wait_recv()

                near_far(t, False, lambda: wo_whole(t).wait_recv(), take_quarters)
        for t in range(1, n_dp):
            rows_copy(t).start()
            grad_copy(t).start()
        with jax.named_scope("ctx_wait"):
            for t in range(1, n_mp):
                ctx_copy(t).wait_recv()
        with jax.named_scope("mix"):
            for c in range(pieces):
                own = contract(ctx_all[piece(c), :], wo_all[...], 1, 1)
                total = rows[piece(c), cols(mp, block)].astype(F32) + own
                mix[mp, piece(c), :] = total.astype(BF16)

                for j in range(len(targets)):
                    mix_copy(c, mp, j).start()
                fwd_copy(c, mp).start()

    for load in loads[6:]:
        load.wait()

    def take(c, b, fresh):
        where = cols(b, block)
        wide = mix[b, piece(c), :].astype(F32)
        scaled = (wide * gain[:, where]).astype(BF16)
        both = contract(scaled, ffn_in[:, where], 1, 1)
        squares = jnp.broadcast_to(jnp.sum(wide * wide, axis=1, keepdims=True), (piece_rows, lanes))
        if fresh:
            gate_up[piece(c), :] = both
            square[piece(c), :] = squares
        else:
            gate_up[piece(c), :] += both
            square[piece(c), :] += squares

    place = sec * n_mp + mp
    with jax.named_scope("own_mix"):
        for c in range(pieces):

            @pl.when(is_enc)
            def _():
                fwd_copy(c, mp).wait_recv()

            take(c, mp, True)

    def gather(c):
        for k, b in enumerate(arrivals):

            @pl.when(is_dec)
            def _():
                mix_copy(c, b, 0).wait_recv()
                if hubs and k > 0:

                    @pl.when(is_hub)
                    def _():
                        mix_copy(c, b, 0).start()

                fwd_copy(c, b).start()

            @pl.when(is_enc)
            def _():
                fwd_copy(c, b).wait_recv()

            take(c, b, False)

    def finish(c):
        with jax.named_scope("hidden%d" % c):
            inverse = lax.rsqrt(square[piece(c), :1] / width + norm_eps)
            gate = gate_up[piece(c), :units] * inverse
            up = gate_up[piece(c), units:] * inverse
            unit_level = level[...].astype(F32) * 0.25
            hidden = (jax.nn.gelu(gate, approximate=True) * up * unit_level).astype(BF16)
            hid_own[piece(c), :] = hidden
            hid_copy(c).start()
            if c == 0:
                down_copy.wait_recv()
            hid_copy(c).wait_recv()
        with jax.named_scope("down%d" % c):

            def product(b):
                where = cols(b, share)
                own = contract(hidden, down_own[:, where], 1, 0)
                return own + contract(hid_other[piece(c), :], down_other[:, where], 1, 0)

            for k in reversed(range(n_mp - 1)):
                own = product(arrivals[k])
                fold_send[k, piece(c), :] = own.astype(BF16)
                if not hubs or k == 0:
                    fold_copy(c, k).start()
                else:
                    partial[k, piece(c), :] = own

                    @pl.when(jnp.logical_not(is_hub))
                    def _():
                        fold_copy(c, k).start()

            there = cols(lax.rem(place, 2), share)
            partial[0, piece(c), :] = product(mp) + mix[place // 2, piece(c), there].astype(F32)

    def combine(c):
        if hubs:

            @pl.when(is_hub)
            def _():
                for k in range(n_mp - 2, 0, -1):
                    fold_in(c, k + 1).wait_recv()
                    total = partial[k, piece(c), :] + fold_recv[k + 1, piece(c), :].astype(F32)
                    fold_send[k, piece(c), :] = total.astype(BF16)
                    fold_copy(c, k).start()

    for c in range(pieces):
        with jax.named_scope("gather%d" % c):
            gather(c)
        finish(c)
        if c:
            with jax.named_scope("combine%d" % (c - 1)):
                combine(c - 1)
    with jax.named_scope("combine%d" % (pieces - 1)):
        combine(pieces - 1)

    own_rows.wait()

    @pl.when(is_dec)
    def _():
        own_grad.wait()

    with jax.named_scope("dp_wait"):
        for t in range(1, n_dp):
            rows_copy(t).wait_recv()

            @pl.when(is_dec)
            def _():
                grad_copy(t).wait_recv()

            g_copy(t).wait_recv()
    with jax.named_scope("weight_grads"):
        flat_rows = rows_all[...].reshape(n_dp * n_rows, cut)
        g_flat = g_all[...].reshape(n_dp * n_rows, 2 * lanes)
        t_left[...] = contract(g_flat[:, :lanes], flat_rows, 0, 0).astype(BF16)

        @pl.when(is_enc)
        def _():
            t_right[...] = contract(g_flat[:, lanes:], flat_rows, 0, 0).astype(BF16)

        @pl.when(is_dec)
        def _():
            flat_grad = grad_all[...].reshape(n_dp * n_rows, cut)
            t_right[...] = contract(g_flat[:, lanes:], flat_grad, 0, 0).astype(BF16)

        row_id = lax.broadcasted_iota(jnp.int32, (tile, lanes), 0)
        d_id = lax.broadcasted_iota(jnp.int32, (tile, lanes), 1)
        spread = [jnp.where(row_id == 2 * d_id + h, 1.0, 0.0).astype(BF16) for h in range(2)]
        for i in range(cut // lanes):
            some = slice(i * lanes, (i + 1) * lanes)
            heads = [
                jnp.concatenate(
                    [t_left[h * half : (h + 1) * half, some], t_right[h * half : (h + 1) * half, some]],
                    axis=0,
                )
                for h in range(2)
            ]
            woven = contract(spread[0], heads[0], 1, 1) + contract(spread[1], heads[1], 1, 1)
            proj_grads[i * tile : (i + 1) * tile, :] = woven.astype(BF16)

    with jax.named_scope("fold"):
        for c in range(pieces):
            mine = partial[0, piece(c), :]
            for k in range(2 if hubs else n_mp - 1):
                fold_in(c, k).wait_recv()
                mine = mine + fold_recv[k, piece(c), :].astype(F32)
            layer_out[piece(c), :] = mine.astype(BF16)

    with jax.named_scope("drain"):
        down_copy.wait_send()
        for t in range(1, n_dp):
            rows_copy(t).wait_send()
            g_copy(t).wait_send()
        for c in range(pieces):
            hid_copy(c).wait_send()
            for k in range(n_mp - 1):
                fold_copy(c, k).wait_send()

        @pl.when(is_enc)
        def _():
            kv_copy.wait_send()

        @pl.when(is_dec)
        def _():
            gkv_copy.wait_send()
            for t in range(1, n_dp):
                grad_copy(t).wait_send()
            for t in range(1, n_mp):
                near_far(t, True, lambda: wo_whole(t).wait_send(), lambda: wo_copy(t).wait_send())
                ctx_copy(t).wait_send()

                def sent_quarters():
                    for s in range(1, relays):
                        relay_out(t, s).wait_send()

                near_far(t, False, lambda: None, sent_quarters)
            for c in range(pieces):
                fwd_copy(c, mp).wait_send()
                for j in range(len(targets)):
                    mix_copy(c, mp, j).wait_send()
                for k, b in enumerate(arrivals):
                    fwd_copy(c, b).wait_send()
                    if hubs and k > 0:

                        @pl.when(is_hub)
                        def _():
                            mix_copy(c, b, 0).wait_send()


def hand_over(a, b, a_out, b_out):
    a_out[...] = a[...]
    b_out[...] = b[...]


def on_device(
    n_dp,
    n_mp,
    section_rows,
    proj_weights,
    out_grad,
    ffn_gain,
    ffn_in,
    ffn_out,
    grow_level,
    dec_seg,
    enc_seg,
):
    rows = section_rows[0]
    n_rows, width = rows.shape
    heads, lanes = proj_weights.shape[2:]
    weight = proj_weights.reshape(width * heads, lanes)
    units = ffn_out.shape[0]
    gates = jnp.transpose(ffn_in, (1, 2, 0)).reshape(2 * units, width)
    block, share, cut = width // n_mp, width // (2 * n_mp), width // n_dp
    relays = math.gcd(n_dp, most_relays)
    vmem = pl.BlockSpec(memory_space=pltpu.VMEM)

    def sems(*shape):
        return pltpu.SemaphoreType.DMA(shape)

    operands = (
        rows,
        weight,
        out_grad,
        ffn_gain[None],
        gates,
        ffn_out,
        grow_level[None],
        dec_seg,
        enc_seg,
    )
    layer_out, grads = pl.pallas_call(
        functools.partial(body, n_dp, n_mp),
        out_shape=(
            jax.ShapeDtypeStruct((n_rows, share), BF16),
            jax.ShapeDtypeStruct((cut * heads, lanes), BF16),
        ),
        in_specs=[pl.BlockSpec(memory_space=pltpu.MemorySpace.HBM)] * 9,
        out_specs=(vmem, vmem),
        scratch_shapes=[pltpu.VMEM(a.shape, a.dtype) for a in operands if a is not ffn_out]
        + [
            pltpu.VMEM((units, width // 2), BF16),
            pltpu.VMEM((units, width // 2), BF16),
            pltpu.VMEM((width, lanes), BF16),
            pltpu.VMEM((width, lanes), BF16),
            pltpu.VMEM((2, n_rows, lanes), BF16),
            pltpu.VMEM((2, n_rows, lanes), BF16),
            pltpu.VMEM((block, n_mp * lanes), BF16),
            pltpu.VMEM((n_rows, n_mp * lanes), BF16),
            pltpu.VMEM((n_dp, n_rows, cut), BF16),
            pltpu.VMEM((n_dp, n_rows, cut), BF16),
            pltpu.VMEM((n_rows, 2 * lanes), BF16),
            pltpu.VMEM((n_dp, n_rows, 2 * lanes), BF16),
            pltpu.VMEM((n_mp, n_rows, block), BF16),
            pltpu.VMEM((n_rows, 2 * units), F32),
            pltpu.VMEM((n_rows, lanes), F32),
            pltpu.VMEM((n_rows, units), BF16),
            pltpu.VMEM((n_rows, units), BF16),
            pltpu.VMEM((n_mp, n_rows, share), F32),
            pltpu.VMEM((n_mp, n_rows, share), BF16),
            pltpu.VMEM((n_mp, n_rows, share), BF16),
            pltpu.VMEM((lanes, cut), BF16),
            pltpu.VMEM((lanes, cut), BF16),
            sems(2, n_dp),
            sems(2, n_dp),
            sems(2, n_dp),
            sems(2, n_mp),
            sems(2, n_mp, relays),
            sems(2, n_mp),
            sems(n_mp, pieces, n_mp),
            sems(pieces, n_mp),
            sems(2, pieces, n_mp),
            sems(2, pieces),
            sems(pieces, n_mp),
            sems(pieces, n_mp),
            sems(2),
            sems(2),
            sems(2),
            sems(n_mp),
            sems(8),
            sems(2),
        ],
        compiler_params=pltpu.CompilerParams(
            collective_id=0, has_side_effects=True, vmem_limit_bytes=67043328
        ),
    )(*operands)
    layer_out, grads = pl.pallas_call(
        hand_over,
        out_shape=(
            jax.ShapeDtypeStruct(layer_out.shape, BF16),
            jax.ShapeDtypeStruct(grads.shape, BF16),
        ),
        in_specs=[vmem] * 2,
        out_specs=(vmem, vmem),
        compiler_params=pltpu.CompilerParams(vmem_limit_bytes=67043328),
    )(layer_out, grads)
    return (layer_out, grads.reshape(1, cut, heads, lanes))


def solution(mesh):
    in_specs = (
        P("sec", "dp", None),
        P("sec", None, "mp", None),
        P("dp", None),
        P(),
        P(None, None, ("sec", "mp")),
        P(("sec", "mp"), None),
        P(("sec", "mp")),
        P("dp", None),
        P("dp", None),
    )
    out_specs = (P("dp", ("sec", "mp")), P("sec", "dp", "mp", None))
    return jax.shard_map(
        functools.partial(on_device, mesh.shape["dp"], mesh.shape["mp"]),
        mesh=mesh,
        in_specs=in_specs,
        out_specs=out_specs,
        check_vma=False,
    )
```

```python
import functools
import math

import jax
import jax.numpy as jnp
from jax import lax
from jax.experimental import pallas as pl
from jax.experimental.pallas import tpu as pltpu
from jax.sharding import PartitionSpec as P

norm_eps = 1e-06
eighths = (4, 4)
eager = True
piped = False
fold_hubs = True
mix_hubs = False
pieces = len(eighths)
most_relays = 4
F32 = jnp.float32
BF16 = jnp.bfloat16


def contract(left, right, left_dim, right_dim):
    dims = (((left_dim,), (right_dim,)), ((), ()))
    return lax.dot_general(left, right, dims, preferred_element_type=F32)


def remote(src, dst, send, recv, device):
    return pltpu.make_async_remote_copy(
        src_ref=src,
        dst_ref=dst,
        send_sem=send,
        recv_sem=recv,
        device_id=device,
        device_id_type=pl.DeviceIdType.MESH,
    )


def body(
    n_dp,
    n_mp,
    rows_hbm,
    weight_hbm,
    grad_hbm,
    gain_hbm,
    ffn_in_hbm,
    ffn_out_hbm,
    level_hbm,
    dec_seg_hbm,
    enc_seg_hbm,
    layer_out,
    proj_grads,
    rows,
    weight,
    grad,
    gain,
    ffn_in,
    level,
    dec_seg,
    enc_seg,
    down_own,
    down_other,
    w_left,
    w_right,
    kv_send,
    kv_recv,
    wo_all,
    ctx_all,
    rows_all,
    grad_all,
    g_send,
    g_all,
    mix,
    gate_up,
    square,
    hid_own,
    hid_other,
    partial,
    fold_send,
    fold_recv,
    t_left,
    t_right,
    rows_sem,
    grad_sem,
    g_sem,
    wo_sem,
    relay_sem,
    ctx_sem,
    mix_send,
    mix_recv,
    fwd_sem,
    hid_sem,
    fold_sem,
    fold_got,
    kv_sem,
    gkv_sem,
    down_sem,
    weight_sem,
    load_sem,
    slot_sem,
):
    sec = lax.axis_index("sec")
    dp = lax.axis_index("dp")
    mp = lax.axis_index("mp")
    n_rows, width = rows.shape
    lanes = weight.shape[1]
    half = lanes // 2
    block = width // n_mp
    share = width // (2 * n_mp)
    cut = width // n_dp
    units = down_own.shape[0]
    hubs = n_mp == 4 and fold_hubs
    passing = n_mp == 4 and mix_hubs
    if n_mp == 4:
        hub = mp * (3 - mp) // 2
        mate = mp + 1 - 2 * lax.rem(mp, 2)
        far_hub = 3 - mp * hub - mate * (1 - hub)
        far_end = 3 - mate * hub - mp * (1 - hub)
        is_hub = hub == 1
    if hubs:
        arrivals = [mate, far_hub, far_end]
    else:
        arrivals = [lax.rem(mp + n_mp - t, n_mp) for t in range(1, n_mp)]
    if passing:
        targets = [mate, 2 - mp // 2]
        sequence = [
            hub * far_hub + (1 - hub) * mate,
            hub * far_end + (1 - hub) * far_hub,
            hub * mate + (1 - hub) * far_end,
        ]
    else:
        targets = [lax.rem(mp + t, n_mp) for t in range(1, n_mp)]
        sequence = [lax.rem(mp + n_mp - t, n_mp) for t in range(1, n_mp)]
    starts = [sum(eighths[:c]) * n_rows // 8 for c in range(pieces + 1)]
    relays = math.gcd(n_dp, most_relays)
    part = block // relays
    turn = lax.rem(dp, relays)
    is_dec = sec == 1
    is_enc = sec == 0
    other = {"sec": 1 - sec}

    def dp_at(t):
        return lax.rem(dp + t, n_dp)

    def mp_at(t):
        return lax.rem(mp + t, n_mp)

    def turn_at(s):
        return lax.rem(turn + s, relays)

    def cols(index, size):
        return pl.ds(pl.multiple_of(index * size, size), size)

    def piece(c):
        return pl.ds(starts[c], starts[c + 1] - starts[c])

    def signal(device):
        pl.semaphore_signal(barrier, inc=1, device_id=device, device_id_type=pl.DeviceIdType.MESH)

    def weight_load(t):
        where = cols(mp_at(t), 2 * block)
        return pltpu.make_async_copy(
            weight_hbm.at[where, :], weight.at[where, :], weight_sem.at[t]
        )

    pairs = (
        (rows_hbm, rows),
        (grad_hbm, grad),
        (dec_seg_hbm, dec_seg),
        (enc_seg_hbm, enc_seg),
        (gain_hbm, gain),
        (level_hbm, level),
        (ffn_in_hbm, ffn_in),
        (ffn_out_hbm.at[:, cols(sec, width // 2)], down_own),
    )
    loads = [pltpu.make_async_copy(a, b, load_sem.at[i]) for i, (a, b) in enumerate(pairs)]
    own_rows = pltpu.make_async_copy(rows_hbm.at[:, cols(dp, cut)], rows_all.at[0], slot_sem.at[0])
    own_grad = pltpu.make_async_copy(grad_hbm.at[:, cols(dp, cut)], grad_all.at[0], slot_sem.at[1])

    def rows_copy(t):
        to = dp_at(t)
        return remote(
            rows_hbm.at[:, cols(to, cut)], rows_all.at[t], rows_sem.at[0, t], rows_sem.at[1, t], {"dp": to}
        )

    def grad_copy(t):
        to = dp_at(t)
        return remote(
            grad_hbm.at[:, cols(to, cut)], grad_all.at[t], grad_sem.at[0, t], grad_sem.at[1, t], {"dp": to}
        )

    def g_copy(t):
        return remote(
            g_all.at[0], g_all.at[t], g_sem.at[0, t], g_sem.at[1, t], {"dp": dp_at(t)}
        )

    def slot(t):
        return slice(t * lanes, (t + 1) * lanes)

    def adjacent(t, sending):
        if t == 1:
            return mp < n_mp - 1 if sending else mp > 0
        return mp > 0 if sending else mp < n_mp - 1

    def near_far(t, sending, near, far):
        if 1 < t < n_mp - 1:
            far()
        else:
            pl.when(adjacent(t, sending))(near)
            pl.when(jnp.logical_not(adjacent(t, sending)))(far)

    def wo_copy(t):
        to = mp_at(t)
        return remote(
            w_right.at[cols(to * relays + turn, part), :],
            wo_all.at[cols(turn, part), slot(t)],
            wo_sem.at[0, t],
            wo_sem.at[1, t],
            {"mp": to},
        )

    def wo_whole(t):
        to = mp_at(t)
        return remote(
            w_right.at[cols(to, block), :],
            wo_all.at[:, slot(t)],
            wo_sem.at[0, t],
            wo_sem.at[1, t],
            {"mp": to},
        )

    def relay_out(t, s):
        ref = wo_all.at[cols(turn, part), slot(t)]
        to = {"dp": dp - turn + turn_at(s)}
        return remote(ref, ref, relay_sem.at[0, t, s], relay_sem.at[1, t, s], to)

    def relay_in(t, s):
        ref = wo_all.at[cols(turn_at(relays - s), part), slot(t)]
        to = {"dp": dp - turn + turn_at(s)}
        return remote(ref, ref, relay_sem.at[0, t, s], relay_sem.at[1, t, s], to)

    def ctx_copy(t):
        return remote(
            ctx_all.at[:, slot(0)],
            ctx_all.at[:, slot(t)],
            ctx_sem.at[0, t],
            ctx_sem.at[1, t],
            {"mp": mp_at(t)},
        )

    def mix_copy(c, b, j):
        ref = mix.at[b, piece(c), :]
        return remote(ref, ref, mix_send.at[j, c, b], mix_recv.at[c, b], {"mp": targets[j]})

    def fwd_copy(c, b):
        ref = mix.at[b, piece(c), :]
        return remote(ref, ref, fwd_sem.at[0, c, b], fwd_sem.at[1, c, b], other)

    def hid_copy(c):
        return remote(
            hid_own.at[piece(c), :], hid_other.at[piece(c), :], hid_sem.at[0, c], hid_sem.at[1, c], other
        )

    def fold_copy(c, k):
        if hubs:
            into = 1 + (1 - hub) * k if k else 0
            to = hub * arrivals[k] + (1 - hub) * mate
        else:
            into, to = k, arrivals[k]
        return remote(
            fold_send.at[k, piece(c), :],
            fold_recv.at[into, piece(c), :],
            fold_sem.at[c, k],
            fold_got.at[c, into],
            {"mp": to},
        )

    def fold_in(c, k):
        return remote(
            fold_send.at[0, piece(c), :],
            fold_recv.at[k, piece(c), :],
            fold_sem.at[c, 0],
            fold_got.at[c, k],
            {"mp": arrivals[0]},
        )

    def send_own(c):
        for j in range(len(targets)):
            mix_copy(c, mp, j).start()

    kv_copy = remote(kv_send, kv_recv, kv_sem.at[0], kv_sem.at[1], other)
    gkv_copy = remote(g_send, g_all.at[0], gkv_sem.at[0], gkv_sem.at[1], other)
    down_copy = remote(
        ffn_out_hbm.at[:, cols(1 - sec, width // 2)], down_other, down_sem.at[0], down_sem.at[1], other
    )

    order = list(range(2, n_mp - 1)) + [1, n_mp - 1, 0]
    with jax.named_scope("signals"):
        barrier = pltpu.get_barrier_semaphore()
        for t in order:
            weight_load(t).start()
        for load in loads[:1]:
            load.start()
        signal(other)
        for t in range(1, n_dp):
            signal({"dp": dp_at(t)})
        for t in range(1, n_mp):
            signal({"mp": mp_at(t)})

    tile = 2 * lanes
    out_id = lax.broadcasted_iota(jnp.int32, (tile, tile), 0)
    in_id = lax.broadcasted_iota(jnp.int32, (tile, tile), 1)
    wanted = jnp.where(out_id < lanes, 2 * out_id, 2 * (out_id - lanes) + 1)
    pick = jnp.where(in_id == wanted, 1.0, 0.0).astype(BF16)
    first = lax.broadcasted_iota(jnp.int32, (lanes, lanes), 1) < half

    for t in order:
        with jax.named_scope("split%d" % t):
            begin = mp_at(t) * block
            weight_load(t).wait()
            for i in range(block // lanes):
                d = pl.multiple_of(begin + i * lanes, lanes)
                two = contract(pick, weight[pl.ds(pl.multiple_of(2 * d, tile), tile), :], 1, 0)
                one, second = two[:lanes], two[lanes:]
                w_left[pl.ds(d, lanes), :] = jnp.where(
                    first, one, pltpu.roll(second, half, 1)
                ).astype(BF16)
                w_right[pl.ds(d, lanes), :] = jnp.where(
                    first, pltpu.roll(one, half, 1), second
                ).astype(BF16)
        if t == order[0]:
            for load in loads[1:6]:
                load.start()
            with jax.named_scope("barrier"):
                pl.semaphore_wait(barrier, n_dp + n_mp - 1)
        if t > 0:

            @pl.when(is_dec)
            def _():
                near_far(t, True, lambda: None, lambda: wo_copy(t).start())

    loads[0].wait()

    @pl.when(is_enc)
    def _():
        with jax.named_scope("kv"):
            kv_send[0] = contract(rows[...], w_left[...], 1, 0).astype(BF16)
            kv_send[1] = contract(rows[...], w_right[...], 1, 0).astype(BF16)
            kv_copy.start()

    for load in loads[6:]:
        load.start()
    own_rows.start()
    down_copy.start()
    for load in loads[1:6]:
        load.wait()

    @pl.when(is_dec)
    def _():
        own_grad.start()
        with jax.named_scope("q_gc"):
            wide_q = contract(rows[...], w_left[...], 1, 0)
            wide_gc = contract(grad[...], w_right[...], 1, 0)
            q = wide_q.astype(BF16)
            gc = wide_gc.astype(BF16)
            dec = jnp.transpose(jnp.broadcast_to(dec_seg[...].astype(F32), (n_rows, n_rows)))
            same = dec == jnp.broadcast_to(enc_seg[...].astype(F32), (n_rows, n_rows))
            wo_all[:, slot(0)] = w_right[cols(mp, block), :]
        with jax.named_scope("relay"):
            for t in range(1, n_mp):

                def pass_quarter():
                    wo_copy(t).wait_recv()
                    for s in range(1, relays):
                        relay_out(t, s).start()

                near_far(t, False, lambda: None, pass_quarter)
            for t in (1, n_mp - 1):
                near_far(t, True, lambda: wo_whole(t).start(), lambda: None)
        with jax.named_scope("kv_wait"):
            kv_copy.wait_recv()
        with jax.named_scope("attend"):
            key = kv_recv[0]
            value = kv_recv[1]
            probs, lows, contexts = [], [], []
            for h in range(2):
                mine = first if h == 0 else jnp.logical_not(first)
                scores = contract(jnp.where(mine, wide_q, 0.0).astype(BF16), key, 1, 1)
                scores = jnp.where(same, scores, -1e30)
                scores = jnp.exp(scores - jnp.max(scores, axis=1, keepdims=True))
                prob = scores / jnp.sum(scores, axis=1, keepdims=True)
                low = prob.astype(BF16)
                probs.append(prob)
                lows.append(low)
                contexts.append(contract(low, value, 1, 0))
            context = jnp.where(first, contexts[0], contexts[1]).astype(BF16)
            ctx_all[:, slot(0)] = context
            g_all[0, :, lanes:] = context
            for t in range(1, n_mp):
                ctx_copy(t).start()
        with jax.named_scope("attend_back"):
            gqs, gks, gvs = [], [], []
            for h in range(2):
                mine = first if h == 0 else jnp.logical_not(first)
                grad_prob = contract(jnp.where(mine, wide_gc, 0.0).astype(BF16), value, 1, 1)
                total = jnp.sum(grad_prob * probs[h], axis=1, keepdims=True)
                score = (probs[h] * (grad_prob - total)).astype(BF16)
                gqs.append(contract(score, key, 1, 0))
                gks.append(contract(score, q, 0, 0))
                gvs.append(contract(lows[h], gc, 0, 0))
            g_send[:, :lanes] = jnp.where(first, gks[0], gks[1]).astype(BF16)
            g_send[:, lanes:] = jnp.where(first, gvs[0], gvs[1]).astype(BF16)
            gkv_copy.start()
            g_all[0, :, :lanes] = jnp.where(first, gqs[0], gqs[1]).astype(BF16)

    @pl.when(is_enc)
    def _():
        with jax.named_scope("gkv_wait"):
            gkv_copy.wait_recv()

    @pl.when(is_dec)
    def _():
        with jax.named_scope("wo_wait"):
            for t in range(1, n_mp):

                def take_quarters():
                    for s in range(1, relays):
                        relay_in(t, s).wait_recv()

                near_far(t, False, lambda: wo_whole(t).wait_recv(), take_quarters)
        for t in range(1, n_dp):
            rows_copy(t).start()
            grad_copy(t).start()
            g_copy(t).start()
        with jax.named_scope("ctx_wait"):
            for t in range(1, n_mp):
                ctx_copy(t).wait_recv()
        with jax.named_scope("mix"):
            for c in range(pieces):
                own = contract(ctx_all[piece(c), :], wo_all[...], 1, 1)
                total = rows[piece(c), cols(mp, block)].astype(F32) + own
                mix[mp, piece(c), :] = total.astype(BF16)

                if c == 0 or eager:
                    send_own(c)
                fwd_copy(c, mp).start()

    for load in loads[6:]:
        load.wait()

    def take(c, b, fresh):
        where = cols(b, block)
        wide = mix[b, piece(c), :].astype(F32)
        scaled = (wide * gain[:, where]).astype(BF16)
        both = contract(scaled, ffn_in[:, where], 1, 1)
        squares = jnp.sum(wide * wide, axis=1, keepdims=True)
        squares = jnp.broadcast_to(squares, (wide.shape[0], lanes))
        if fresh:
            gate_up[piece(c), :] = both
            square[piece(c), :] = squares
        else:
            gate_up[piece(c), :] += both
            square[piece(c), :] += squares

    place = sec * n_mp + mp
    def gather(c):
        @pl.when(is_enc)
        def _():
            fwd_copy(c, mp).wait_recv()
            if c == 0:
                for t in range(1, n_dp):
                    rows_copy(t).start()
                    g_copy(t).start()

        take(c, mp, True)
        for k, b in enumerate(sequence):

            @pl.when(is_dec)
            def _():
                mix_copy(c, b, 0).wait_recv()
                if passing and k < 2:

                    @pl.when(is_hub)
                    def _():
                        mix_copy(c, b, 0).start()

                fwd_copy(c, b).start()
                if not eager and c + 1 < pieces and k == min(1, len(arrivals) - 1):
                    send_own(c + 1)

            @pl.when(is_enc)
            def _():
                fwd_copy(c, b).wait_recv()

            take(c, b, False)

    def activate(c):
        with jax.named_scope("hidden%d" % c):
            inverse = lax.rsqrt(square[piece(c), :1] / width + norm_eps)
            gate = gate_up[piece(c), :units] * inverse
            up = gate_up[piece(c), units:] * inverse
            unit_level = level[...].astype(F32) * 0.25
            hidden = (jax.nn.gelu(gate, approximate=True) * up * unit_level).astype(BF16)
            hid_own[piece(c), :] = hidden
            hid_copy(c).start()

    def descend(c):
        with jax.named_scope("hid_wait%d" % c):
            if c == 0:
                down_copy.wait_recv()
            hid_copy(c).wait_recv()
        with jax.named_scope("down%d" % c):
            hidden = hid_own[piece(c), :]

            def product(b):
                where = cols(b, share)
                own = contract(hidden, down_own[:, where], 1, 0)
                return own + contract(hid_other[piece(c), :], down_other[:, where], 1, 0)

            for k in reversed(range(n_mp - 1)):
                own = product(arrivals[k])
                fold_send[k, piece(c), :] = own.astype(BF16)
                if not hubs or k == 0:
                    fold_copy(c, k).start()
                else:
                    partial[k, piece(c), :] = own

                    @pl.when(jnp.logical_not(is_hub))
                    def _():
                        fold_copy(c, k).start()

            there = cols(lax.rem(place, 2), share)
            partial[0, piece(c), :] = product(mp) + mix[place // 2, piece(c), there].astype(F32)

    def combine(c):
        if hubs:

            @pl.when(is_hub)
            def _():
                for k in range(n_mp - 2, 0, -1):
                    fold_in(c, k + 1).wait_recv()
                    total = partial[k, piece(c), :] + fold_recv[k + 1, piece(c), :].astype(F32)
                    fold_send[k, piece(c), :] = total.astype(BF16)
                    fold_copy(c, k).start()

    for c in range(pieces):
        with jax.named_scope("gather%d" % c):
            gather(c)
        activate(c)
        if piped and c > 0:
            descend(c - 1)
        if not piped:
            descend(c)
        if c > 1:
            with jax.named_scope("combine%d" % (c - 2)):
                combine(c - 2)
    if piped:
        descend(pieces - 1)
    for c in range(max(pieces - 2, 0), pieces):
        with jax.named_scope("combine%d" % c):
            combine(c)

    own_rows.wait()

    @pl.when(is_dec)
    def _():
        own_grad.wait()

    with jax.named_scope("dp_wait"):
        for t in range(1, n_dp):
            rows_copy(t).wait_recv()

            @pl.when(is_dec)
            def _():
                grad_copy(t).wait_recv()

            g_copy(t).wait_recv()
    with jax.named_scope("weight_grads"):
        flat_rows = rows_all[...].reshape(n_dp * n_rows, cut)
        g_flat = g_all[...].reshape(n_dp * n_rows, 2 * lanes)
        t_left[...] = contract(g_flat[:, :lanes], flat_rows, 0, 0).astype(BF16)

        @pl.when(is_enc)
        def _():
            t_right[...] = contract(g_flat[:, lanes:], flat_rows, 0, 0).astype(BF16)

        @pl.when(is_dec)
        def _():
            flat_grad = grad_all[...].reshape(n_dp * n_rows, cut)
            t_right[...] = contract(g_flat[:, lanes:], flat_grad, 0, 0).astype(BF16)

        row_id = lax.broadcasted_iota(jnp.int32, (tile, lanes), 0)
        d_id = lax.broadcasted_iota(jnp.int32, (tile, lanes), 1)
        spread = [jnp.where(row_id == 2 * d_id + h, 1.0, 0.0).astype(BF16) for h in range(2)]
        for i in range(cut // lanes):
            some = slice(i * lanes, (i + 1) * lanes)
            heads = [
                jnp.concatenate(
                    [t_left[h * half : (h + 1) * half, some], t_right[h * half : (h + 1) * half, some]],
                    axis=0,
                )
                for h in range(2)
            ]
            woven = contract(spread[0], heads[0], 1, 1) + contract(spread[1], heads[1], 1, 1)
            proj_grads[i * tile : (i + 1) * tile, :] = woven.astype(BF16)

    with jax.named_scope("fold"):
        for c in range(pieces):
            mine = partial[0, piece(c), :]
            for k in range(2 if hubs else n_mp - 1):
                fold_in(c, k).wait_recv()
                mine = mine + fold_recv[k, piece(c), :].astype(F32)
            layer_out[piece(c), :] = mine.astype(BF16)

    with jax.named_scope("drain"):
        down_copy.wait_send()
        for t in range(1, n_dp):
            rows_copy(t).wait_send()
            g_copy(t).wait_send()
        for c in range(pieces):
            hid_copy(c).wait_send()
            for k in range(n_mp - 1):
                fold_copy(c, k).wait_send()

        @pl.when(is_enc)
        def _():
            kv_copy.wait_send()

        @pl.when(is_dec)
        def _():
            gkv_copy.wait_send()
            for t in range(1, n_dp):
                grad_copy(t).wait_send()
            for t in range(1, n_mp):
                near_far(t, True, lambda: wo_whole(t).wait_send(), lambda: wo_copy(t).wait_send())
                ctx_copy(t).wait_send()

                def sent_quarters():
                    for s in range(1, relays):
                        relay_out(t, s).wait_send()

                near_far(t, False, lambda: None, sent_quarters)
            for c in range(pieces):
                fwd_copy(c, mp).wait_send()
                for j in range(len(targets)):
                    mix_copy(c, mp, j).wait_send()
                for k, b in enumerate(sequence):
                    fwd_copy(c, b).wait_send()
                    if passing and k < 2:

                        @pl.when(is_hub)
                        def _():
                            mix_copy(c, b, 0).wait_send()


def hand_over(a, b, a_out, b_out, sem):
    copies = [pltpu.make_async_copy(a, a_out, sem.at[0]), pltpu.make_async_copy(b, b_out, sem.at[1])]
    for copy in copies:
        copy.start()
    for copy in copies:
        copy.wait()


def on_device(
    n_dp,
    n_mp,
    section_rows,
    proj_weights,
    out_grad,
    ffn_gain,
    ffn_in,
    ffn_out,
    grow_level,
    dec_seg,
    enc_seg,
):
    rows = section_rows[0]
    n_rows, width = rows.shape
    heads, lanes = proj_weights.shape[2:]
    weight = proj_weights.reshape(width * heads, lanes)
    units = ffn_out.shape[0]
    gates = jnp.transpose(ffn_in, (1, 2, 0)).reshape(2 * units, width)
    block, share, cut = width // n_mp, width // (2 * n_mp), width // n_dp
    relays = math.gcd(n_dp, most_relays)
    vmem = pl.BlockSpec(memory_space=pltpu.VMEM)

    def sems(*shape):
        return pltpu.SemaphoreType.DMA(shape)

    operands = (
        rows,
        weight,
        out_grad,
        ffn_gain[None],
        gates,
        ffn_out,
        grow_level[None],
        dec_seg,
        enc_seg,
    )
    layer_out, grads = pl.pallas_call(
        functools.partial(body, n_dp, n_mp),
        out_shape=(
            pltpu.VMEM((n_rows, share), BF16),
            pltpu.VMEM((cut * heads, lanes), BF16),
        ),
        in_specs=[pl.BlockSpec(memory_space=pltpu.MemorySpace.HBM)] * 9,
        out_specs=(vmem, vmem),
        scratch_shapes=[pltpu.VMEM(a.shape, a.dtype) for a in operands if a is not ffn_out]
        + [
            pltpu.VMEM((units, width // 2), BF16),
            pltpu.VMEM((units, width // 2), BF16),
            pltpu.VMEM((width, lanes), BF16),
            pltpu.VMEM((width, lanes), BF16),
            pltpu.VMEM((2, n_rows, lanes), BF16),
            pltpu.VMEM((2, n_rows, lanes), BF16),
            pltpu.VMEM((block, n_mp * lanes), BF16),
            pltpu.VMEM((n_rows, n_mp * lanes), BF16),
            pltpu.VMEM((n_dp, n_rows, cut), BF16),
            pltpu.VMEM((n_dp, n_rows, cut), BF16),
            pltpu.VMEM((n_rows, 2 * lanes), BF16),
            pltpu.VMEM((n_dp, n_rows, 2 * lanes), BF16),
            pltpu.VMEM((n_mp, n_rows, block), BF16),
            pltpu.VMEM((n_rows, 2 * units), F32),
            pltpu.VMEM((n_rows, lanes), F32),
            pltpu.VMEM((n_rows, units), BF16),
            pltpu.VMEM((n_rows, units), BF16),
            pltpu.VMEM((n_mp, n_rows, share), F32),
            pltpu.VMEM((n_mp, n_rows, share), BF16),
            pltpu.VMEM((n_mp, n_rows, share), BF16),
            pltpu.VMEM((lanes, cut), BF16),
            pltpu.VMEM((lanes, cut), BF16),
            sems(2, n_dp),
            sems(2, n_dp),
            sems(2, n_dp),
            sems(2, n_mp),
            sems(2, n_mp, relays),
            sems(2, n_mp),
            sems(n_mp, pieces, n_mp),
            sems(pieces, n_mp),
            sems(2, pieces, n_mp),
            sems(2, pieces),
            sems(pieces, n_mp),
            sems(pieces, n_mp),
            sems(2),
            sems(2),
            sems(2),
            sems(n_mp),
            sems(8),
            sems(2),
        ],
        compiler_params=pltpu.CompilerParams(
            collective_id=0, has_side_effects=True, vmem_limit_bytes=58 << 20
        ),
    )(*operands)
    layer_out, grads = pl.pallas_call(
        hand_over,
        out_shape=(
            jax.ShapeDtypeStruct(layer_out.shape, BF16),
            jax.ShapeDtypeStruct(grads.shape, BF16),
        ),
        in_specs=[vmem] * 2,
        out_specs=(pl.BlockSpec(memory_space=pl.ANY),) * 2,
        scratch_shapes=[pltpu.SemaphoreType.DMA((2,))],
    )(*(pltpu.with_memory_space_constraint(a, pltpu.VMEM) for a in (layer_out, grads)))
    return (layer_out, grads.reshape(1, cut, heads, lanes))


def solution(mesh):
    in_specs = (
        P("sec", "dp", None),
        P("sec", None, "mp", None),
        P("dp", None),
        P(),
        P(None, None, ("sec", "mp")),
        P(("sec", "mp"), None),
        P(("sec", "mp")),
        P("dp", None),
        P("dp", None),
    )
    out_specs = (P("dp", ("sec", "mp")), P("sec", "dp", "mp", None))
    return jax.shard_map(
        functools.partial(on_device, mesh.shape["dp"], mesh.shape["mp"]),
        mesh=mesh,
        in_specs=in_specs,
        out_specs=out_specs,
        check_vma=False,
    )
```

```python
import functools
import math

import jax
import jax.numpy as jnp
from jax import lax
from jax.experimental import pallas as pl
from jax.experimental.pallas import tpu as pltpu
from jax.sharding import PartitionSpec as P

norm_eps = 1e-06
eighths = (4, 4)
eager = True
piped = False
fold_hubs = True
mix_hubs = False
pieces = len(eighths)
most_relays = 4
F32 = jnp.float32
BF16 = jnp.bfloat16


def contract(left, right, left_dim, right_dim):
    dims = (((left_dim,), (right_dim,)), ((), ()))
    return lax.dot_general(left, right, dims, preferred_element_type=F32)


def remote(src, dst, send, recv, device):
    return pltpu.make_async_remote_copy(
        src_ref=src,
        dst_ref=dst,
        send_sem=send,
        recv_sem=recv,
        device_id=device,
        device_id_type=pl.DeviceIdType.MESH,
    )


def body(
    n_dp,
    n_mp,
    rows_hbm,
    weight_hbm,
    grad_hbm,
    gain_hbm,
    ffn_in_hbm,
    ffn_out_hbm,
    level_hbm,
    dec_seg_hbm,
    enc_seg_hbm,
    layer_out,
    proj_grads,
    rows,
    weight,
    grad,
    gain,
    ffn_in,
    level,
    dec_seg,
    enc_seg,
    down_own,
    down_other,
    w_left,
    w_right,
    kv_send,
    kv_recv,
    wo_all,
    ctx_all,
    rows_all,
    grad_all,
    g_send,
    g_all,
    mix,
    gate_up,
    square,
    hid_own,
    hid_other,
    partial,
    fold_send,
    fold_recv,
    t_left,
    t_right,
    rows_sem,
    grad_sem,
    g_sem,
    wo_sem,
    relay_sem,
    ctx_sem,
    mix_send,
    mix_recv,
    fwd_sem,
    hid_sem,
    fold_sem,
    fold_got,
    kv_sem,
    gkv_sem,
    down_sem,
    weight_sem,
    load_sem,
    slot_sem,
):
    sec = lax.axis_index("sec")
    dp = lax.axis_index("dp")
    mp = lax.axis_index("mp")
    n_rows, width = rows.shape
    lanes = weight.shape[1]
    half = lanes // 2
    block = width // n_mp
    share = width // (2 * n_mp)
    cut = width // n_dp
    units = down_own.shape[0]
    hubs = n_mp == 4 and fold_hubs
    passing = n_mp == 4 and mix_hubs
    if n_mp == 4:
        hub = mp * (3 - mp) // 2
        mate = mp + 1 - 2 * lax.rem(mp, 2)
        far_hub = 3 - mp * hub - mate * (1 - hub)
        far_end = 3 - mate * hub - mp * (1 - hub)
        is_hub = hub == 1
    if hubs:
        arrivals = [mate, far_hub, far_end]
    else:
        arrivals = [lax.rem(mp + n_mp - t, n_mp) for t in range(1, n_mp)]
    if passing:
        targets = [mate, 2 - mp // 2]
        sequence = [
            hub * far_hub + (1 - hub) * mate,
            hub * far_end + (1 - hub) * far_hub,
            hub * mate + (1 - hub) * far_end,
        ]
    elif n_mp == 4:
        targets = [far_end, far_hub, mate]
        sequence = [mate, far_hub, far_end]
    else:
        targets = [lax.rem(mp + t, n_mp) for t in range(1, n_mp)]
        sequence = [lax.rem(mp + n_mp - t, n_mp) for t in range(1, n_mp)]
    starts = [sum(eighths[:c]) * n_rows // 8 for c in range(pieces + 1)]
    relays = math.gcd(n_dp, most_relays)
    part = block // relays
    turn = lax.rem(dp, relays)
    is_dec = sec == 1
    is_enc = sec == 0
    other = {"sec": 1 - sec}

    def dp_at(t):
        return lax.rem(dp + t, n_dp)

    def mp_at(t):
        return lax.rem(mp + t, n_mp)

    def turn_at(s):
        return lax.rem(turn + s, relays)

    def cols(index, size):
        return pl.ds(pl.multiple_of(index * size, size), size)

    def piece(c):
        return pl.ds(starts[c], starts[c + 1] - starts[c])

    def signal(device):
        pl.semaphore_signal(barrier, inc=1, device_id=device, device_id_type=pl.DeviceIdType.MESH)

    def weight_load(t):
        where = cols(mp_at(t), 2 * block)
        return pltpu.make_async_copy(
            weight_hbm.at[where, :], weight.at[where, :], weight_sem.at[t]
        )

    pairs = (
        (rows_hbm, rows),
        (grad_hbm, grad),
        (dec_seg_hbm, dec_seg),
        (enc_seg_hbm, enc_seg),
        (gain_hbm, gain),
        (level_hbm, level),
        (ffn_in_hbm, ffn_in),
        (ffn_out_hbm.at[:, cols(sec, width // 2)], down_own),
    )
    loads = [pltpu.make_async_copy(a, b, load_sem.at[i]) for i, (a, b) in enumerate(pairs)]
    own_rows = pltpu.make_async_copy(rows_hbm.at[:, cols(dp, cut)], rows_all.at[0], slot_sem.at[0])
    own_grad = pltpu.make_async_copy(grad_hbm.at[:, cols(dp, cut)], grad_all.at[0], slot_sem.at[1])

    def rows_copy(t):
        to = dp_at(t)
        return remote(
            rows_hbm.at[:, cols(to, cut)], rows_all.at[t], rows_sem.at[0, t - 1], rows_sem.at[1, t - 1], {"dp": to}
        )

    def grad_copy(t):
        to = dp_at(t)
        return remote(
            grad_hbm.at[:, cols(to, cut)], grad_all.at[t], grad_sem.at[0, t - 1], grad_sem.at[1, t - 1], {"dp": to}
        )

    def g_copy(t):
        return remote(
            g_all.at[0], g_all.at[t], g_sem.at[0, t - 1], g_sem.at[1, t - 1], {"dp": dp_at(t)}
        )

    def slot(t):
        return slice(t * lanes, (t + 1) * lanes)

    def adjacent(t, sending):
        if t == 1:
            return mp < n_mp - 1 if sending else mp > 0
        return mp > 0 if sending else mp < n_mp - 1

    def near_far(t, sending, near, far):
        if 1 < t < n_mp - 1:
            far()
        else:
            pl.when(adjacent(t, sending))(near)
            pl.when(jnp.logical_not(adjacent(t, sending)))(far)

    def wo_copy(t):
        to = mp_at(t)
        return remote(
            w_right.at[cols(to * relays + turn, part), :],
            wo_all.at[cols(turn, part), slot(t)],
            wo_sem.at[0, t - 1],
            wo_sem.at[1, t - 1],
            {"mp": to},
        )

    def wo_whole(t):
        to = mp_at(t)
        return remote(
            w_right.at[cols(to, block), :],
            wo_all.at[:, slot(t)],
            wo_sem.at[0, t - 1],
            wo_sem.at[1, t - 1],
            {"mp": to},
        )

    def relay_out(t, s):
        ref = wo_all.at[cols(turn, part), slot(t)]
        to = {"dp": dp - turn + turn_at(s)}
        return remote(ref, ref, relay_sem.at[0, t - 1, s - 1], relay_sem.at[1, t - 1, s - 1], to)

    def relay_in(t, s):
        ref = wo_all.at[cols(turn_at(relays - s), part), slot(t)]
        to = {"dp": dp - turn + turn_at(s)}
        return remote(ref, ref, relay_sem.at[0, t - 1, s - 1], relay_sem.at[1, t - 1, s - 1], to)

    def ctx_copy(t):
        return remote(
            ctx_all.at[:, slot(0)],
            ctx_all.at[:, slot(t)],
            ctx_sem.at[0, t - 1],
            ctx_sem.at[1, t - 1],
            {"mp": mp_at(t)},
        )

    def mix_copy(c, b, j):
        ref = mix.at[b, piece(c), :]
        return remote(ref, ref, mix_send.at[j, c], mix_recv.at[c, b], {"mp": targets[j]})

    def fwd_copy(c, b):
        ref = mix.at[b, piece(c), :]
        return remote(ref, ref, fwd_sem.at[0, c, b], fwd_sem.at[1, c, b], other)

    def hid_copy(c):
        return remote(
            hid_own.at[piece(c), :], hid_other.at[piece(c), :], hid_sem.at[0, c], hid_sem.at[1, c], other
        )

    def fold_copy(c, k):
        if hubs:
            into = 1 + (1 - hub) * k if k else 0
            to = hub * arrivals[k] + (1 - hub) * mate
        else:
            into, to = k, arrivals[k]
        return remote(
            fold_send.at[k, piece(c), :],
            fold_recv.at[into, piece(c), :],
            fold_sem.at[c, k],
            fold_got.at[c, into],
            {"mp": to},
        )

    def fold_in(c, k):
        return remote(
            fold_send.at[0, piece(c), :],
            fold_recv.at[k, piece(c), :],
            fold_sem.at[c, 0],
            fold_got.at[c, k],
            {"mp": arrivals[0]},
        )

    def send_own(c):
        for j in range(len(targets)):
            mix_copy(c, mp, j).start()

    kv_copy = remote(kv_send, kv_recv, kv_sem.at[0], kv_sem.at[1], other)
    gkv_copy = remote(g_send, g_all.at[0], gkv_sem.at[0], gkv_sem.at[1], other)
    down_copy = remote(
        ffn_out_hbm.at[:, cols(1 - sec, width // 2)], down_other, down_sem.at[0], down_sem.at[1], other
    )

    order = list(range(2, n_mp - 1)) + [1, n_mp - 1, 0]
    if n_dp == 4:
        beside = 1 + 2 * lax.rem(dp, 2)
        near_dp, far_dp = [beside, 2], [4 - beside]
    else:
        near_dp, far_dp = [1], list(range(2, n_dp))
    with jax.named_scope("signals"):
        barrier = pltpu.get_barrier_semaphore()
        for t in order:
            weight_load(t).start()
        for load in loads[:1]:
            load.start()
        signal(other)
        for t in range(1, n_dp):
            signal({"dp": dp_at(t)})
        for t in range(1, n_mp):
            signal({"mp": mp_at(t)})

    tile = 2 * lanes
    out_id = lax.broadcasted_iota(jnp.int32, (tile, tile), 0)
    in_id = lax.broadcasted_iota(jnp.int32, (tile, tile), 1)
    wanted = jnp.where(out_id < lanes, 2 * out_id, 2 * (out_id - lanes) + 1)
    pick = jnp.where(in_id == wanted, 1.0, 0.0).astype(BF16)
    first = lax.broadcasted_iota(jnp.int32, (lanes, lanes), 1) < half

    for t in order:
        with jax.named_scope("split%d" % t):
            begin = mp_at(t) * block
            weight_load(t).wait()
            for i in range(block // lanes):
                d = pl.multiple_of(begin + i * lanes, lanes)
                two = contract(pick, weight[pl.ds(pl.multiple_of(2 * d, tile), tile), :], 1, 0)
                one, second = two[:lanes], two[lanes:]
                w_left[pl.ds(d, lanes), :] = jnp.where(
                    first, one, pltpu.roll(second, half, 1)
                ).astype(BF16)
                w_right[pl.ds(d, lanes), :] = jnp.where(
                    first, pltpu.roll(one, half, 1), second
                ).astype(BF16)
        if t == order[0]:
            for load in loads[1:6]:
                load.start()
            with jax.named_scope("barrier"):
                pl.semaphore_wait(barrier, n_dp + n_mp - 1)

            @pl.when(is_enc)
            def _():
                for t in near_dp:
                    rows_copy(t).start()

        if t > 0:

            @pl.when(is_dec)
            def _():
                near_far(t, True, lambda: None, lambda: wo_copy(t).start())

    loads[0].wait()

    @pl.when(is_enc)
    def _():
        with jax.named_scope("kv"):
            kv_send[0] = contract(rows[...], w_left[...], 1, 0).astype(BF16)
            kv_send[1] = contract(rows[...], w_right[...], 1, 0).astype(BF16)
            kv_copy.start()

    for load in loads[6:]:
        load.start()
    own_rows.start()
    down_copy.start()
    for load in loads[1:6]:
        load.wait()

    @pl.when(is_dec)
    def _():
        own_grad.start()
        for t in (1, n_mp - 1):
            near_far(t, True, lambda: wo_whole(t).start(), lambda: None)
        with jax.named_scope("q_gc"):
            wide_q = contract(rows[...], w_left[...], 1, 0)
            wide_gc = contract(grad[...], w_right[...], 1, 0)
            q = wide_q.astype(BF16)
            gc = wide_gc.astype(BF16)
            dec = jnp.transpose(jnp.broadcast_to(dec_seg[...].astype(F32), (n_rows, n_rows)))
            same = dec == jnp.broadcast_to(enc_seg[...].astype(F32), (n_rows, n_rows))
            wo_all[:, slot(0)] = w_right[cols(mp, block), :]
        with jax.named_scope("relay"):
            for t in order[:-1]:

                def pass_quarter():
                    wo_copy(t).wait_recv()
                    for s in range(1, relays):
                        relay_out(t, s).start()

                near_far(t, False, lambda: None, pass_quarter)
        with jax.named_scope("kv_wait"):
            kv_copy.wait_recv()
        with jax.named_scope("attend"):
            key = kv_recv[0]
            value = kv_recv[1]
            probs, lows, contexts = [], [], []
            for h in range(2):
                mine = first if h == 0 else jnp.logical_not(first)
                scores = contract(jnp.where(mine, wide_q, 0.0).astype(BF16), key, 1, 1)
                scores = jnp.where(same, scores, -1e30)
                scores = jnp.exp(scores - jnp.max(scores, axis=1, keepdims=True))
                prob = scores / jnp.sum(scores, axis=1, keepdims=True)
                low = prob.astype(BF16)
                probs.append(prob)
                lows.append(low)
                contexts.append(contract(low, value, 1, 0))
            context = jnp.where(first, contexts[0], contexts[1]).astype(BF16)
            ctx_all[:, slot(0)] = context
            g_all[0, :, lanes:] = context
            for t in range(1, n_mp):
                ctx_copy(t).start()
        with jax.named_scope("attend_back"):
            gqs, gks, gvs = [], [], []
            for h in range(2):
                mine = first if h == 0 else jnp.logical_not(first)
                grad_prob = contract(jnp.where(mine, wide_gc, 0.0).astype(BF16), value, 1, 1)
                total = jnp.sum(grad_prob * probs[h], axis=1, keepdims=True)
                score = (probs[h] * (grad_prob - total)).astype(BF16)
                gqs.append(contract(score, key, 1, 0))
                gks.append(contract(score, q, 0, 0))
                gvs.append(contract(lows[h], gc, 0, 0))
            g_send[:, :lanes] = jnp.where(first, gks[0], gks[1]).astype(BF16)
            g_send[:, lanes:] = jnp.where(first, gvs[0], gvs[1]).astype(BF16)
            gkv_copy.start()
            g_all[0, :, :lanes] = jnp.where(first, gqs[0], gqs[1]).astype(BF16)

    @pl.when(is_enc)
    def _():
        with jax.named_scope("gkv_wait"):
            gkv_copy.wait_recv()

    @pl.when(is_dec)
    def _():
        with jax.named_scope("wo_wait"):
            for t in range(1, n_mp):

                def take_quarters():
                    for s in range(1, relays):
                        relay_in(t, s).wait_recv()

                near_far(t, False, lambda: wo_whole(t).wait_recv(), take_quarters)
        for t in range(1, n_dp):
            rows_copy(t).start()
            grad_copy(t).start()
            g_copy(t).start()
        with jax.named_scope("ctx_wait"):
            for t in range(1, n_mp):
                ctx_copy(t).wait_recv()
        with jax.named_scope("mix"):
            for c in range(pieces):
                own = contract(ctx_all[piece(c), :], wo_all[...], 1, 1)
                total = rows[piece(c), cols(mp, block)].astype(F32) + own
                mix[mp, piece(c), :] = total.astype(BF16)

                if c == 0 or eager:
                    send_own(c)
                fwd_copy(c, mp).start()

    for load in loads[6:]:
        load.wait()

    def take(c, b, fresh):
        where = cols(b, block)
        wide = mix[b, piece(c), :].astype(F32)
        scaled = (wide * gain[:, where]).astype(BF16)
        both = contract(scaled, ffn_in[:, where], 1, 1)
        squares = jnp.sum(wide * wide, axis=1, keepdims=True)
        squares = jnp.broadcast_to(squares, (wide.shape[0], lanes))
        if fresh:
            gate_up[piece(c), :] = both
            square[piece(c), :] = squares
        else:
            gate_up[piece(c), :] += both
            square[piece(c), :] += squares

    place = sec * n_mp + mp
    def gather(c):
        @pl.when(is_enc)
        def _():
            fwd_copy(c, mp).wait_recv()
            if c == 0:
                for t in far_dp:
                    rows_copy(t).start()
                for t in range(1, n_dp):
                    g_copy(t).start()

        take(c, mp, True)
        for k, b in enumerate(sequence):

            @pl.when(is_dec)
            def _():
                mix_copy(c, b, 0).wait_recv()
                if passing and k < 2:

                    @pl.when(is_hub)
                    def _():
                        mix_copy(c, b, 0).start()

                fwd_copy(c, b).start()
                if not eager and c + 1 < pieces and k == min(1, len(arrivals) - 1):
                    send_own(c + 1)

            @pl.when(is_enc)
            def _():
                fwd_copy(c, b).wait_recv()

            take(c, b, False)

    def activate(c):
        with jax.named_scope("hidden%d" % c):
            inverse = lax.rsqrt(square[piece(c), :1] / width + norm_eps)
            gate = gate_up[piece(c), :units] * inverse
            up = gate_up[piece(c), units:] * inverse
            unit_level = level[...].astype(F32) * 0.25
            hidden = (jax.nn.gelu(gate, approximate=True) * up * unit_level).astype(BF16)
            hid_own[piece(c), :] = hidden
            hid_copy(c).start()

    def descend(c):
        with jax.named_scope("down_own%d" % c):
            hidden = hid_own[piece(c), :]
            for k in reversed(range(n_mp - 1)):
                partial[k, piece(c), :] = contract(hidden, down_own[:, cols(arrivals[k], share)], 1, 0)
        with jax.named_scope("hid_wait%d" % c):
            if c == 0:
                down_copy.wait_recv()
            hid_copy(c).wait_recv()
        with jax.named_scope("down%d" % c):
            beside_hidden = hid_other[piece(c), :]

            def product(b):
                where = cols(b, share)
                own = contract(hidden, down_own[:, where], 1, 0)
                return own + contract(beside_hidden, down_other[:, where], 1, 0)

            for k in reversed(range(n_mp - 1)):
                other_part = contract(beside_hidden, down_other[:, cols(arrivals[k], share)], 1, 0)
                own = partial[k, piece(c), :] + other_part
                fold_send[k, piece(c), :] = own.astype(BF16)
                if not hubs or k == 0:
                    fold_copy(c, k).start()
                else:
                    partial[k, piece(c), :] = own

                    @pl.when(jnp.logical_not(is_hub))
                    def _():
                        fold_copy(c, k).start()

            there = cols(lax.rem(place, 2), share)
            partial[0, piece(c), :] = product(mp) + mix[place // 2, piece(c), there].astype(F32)

    def combine(c):
        if hubs:

            @pl.when(is_hub)
            def _():
                for k in range(n_mp - 2, 0, -1):
                    fold_in(c, k + 1).wait_recv()
                    total = partial[k, piece(c), :] + fold_recv[k + 1, piece(c), :].astype(F32)
                    fold_send[k, piece(c), :] = total.astype(BF16)
                    fold_copy(c, k).start()

    for c in range(pieces):
        with jax.named_scope("gather%d" % c):
            gather(c)
        activate(c)
        if piped and c > 0:
            descend(c - 1)
        if not piped:
            descend(c)
        if c > 1:
            with jax.named_scope("combine%d" % (c - 2)):
                combine(c - 2)
    if piped:
        descend(pieces - 1)
    for c in range(max(pieces - 2, 0), pieces):
        with jax.named_scope("combine%d" % c):
            combine(c)

    own_rows.wait()

    @pl.when(is_dec)
    def _():
        own_grad.wait()

    with jax.named_scope("dp_wait"):
        for t in range(1, n_dp):
            rows_copy(t).wait_recv()

            @pl.when(is_dec)
            def _():
                grad_copy(t).wait_recv()

            g_copy(t).wait_recv()
    with jax.named_scope("weight_grads"):
        flat_rows = rows_all[...].reshape(n_dp * n_rows, cut)
        g_flat = g_all[...].reshape(n_dp * n_rows, 2 * lanes)
        t_left[...] = contract(g_flat[:, :lanes], flat_rows, 0, 0).astype(BF16)

        @pl.when(is_enc)
        def _():
            t_right[...] = contract(g_flat[:, lanes:], flat_rows, 0, 0).astype(BF16)

        @pl.when(is_dec)
        def _():
            flat_grad = grad_all[...].reshape(n_dp * n_rows, cut)
            t_right[...] = contract(g_flat[:, lanes:], flat_grad, 0, 0).astype(BF16)

        row_id = lax.broadcasted_iota(jnp.int32, (tile, lanes), 0)
        d_id = lax.broadcasted_iota(jnp.int32, (tile, lanes), 1)
        spread = [jnp.where(row_id == 2 * d_id + h, 1.0, 0.0).astype(BF16) for h in range(2)]
        for i in range(cut // lanes):
            some = slice(i * lanes, (i + 1) * lanes)
            heads = [
                jnp.concatenate(
                    [t_left[h * half : (h + 1) * half, some], t_right[h * half : (h + 1) * half, some]],
                    axis=0,
                )
                for h in range(2)
            ]
            woven = contract(spread[0], heads[0], 1, 1) + contract(spread[1], heads[1], 1, 1)
            proj_grads[i * tile : (i + 1) * tile, :] = woven.astype(BF16)

    with jax.named_scope("fold"):
        for c in range(pieces):
            mine = partial[0, piece(c), :]
            for k in range(2 if hubs else n_mp - 1):
                fold_in(c, k).wait_recv()
                mine = mine + fold_recv[k, piece(c), :].astype(F32)
            layer_out[piece(c), :] = mine.astype(BF16)

    with jax.named_scope("drain"):
        down_copy.wait_send()
        for t in range(1, n_dp):
            rows_copy(t).wait_send()
            g_copy(t).wait_send()
        for c in range(pieces):
            hid_copy(c).wait_send()
            for k in range(n_mp - 1):
                fold_copy(c, k).wait_send()

        @pl.when(is_enc)
        def _():
            kv_copy.wait_send()

        @pl.when(is_dec)
        def _():
            gkv_copy.wait_send()
            for t in range(1, n_dp):
                grad_copy(t).wait_send()
            for t in range(1, n_mp):
                near_far(t, True, lambda: wo_whole(t).wait_send(), lambda: wo_copy(t).wait_send())
                ctx_copy(t).wait_send()

                def sent_quarters():
                    for s in range(1, relays):
                        relay_out(t, s).wait_send()

                near_far(t, False, lambda: None, sent_quarters)
            for c in range(pieces):
                fwd_copy(c, mp).wait_send()
                for j in range(len(targets)):
                    mix_copy(c, mp, j).wait_send()
                for k, b in enumerate(sequence):
                    fwd_copy(c, b).wait_send()
                    if passing and k < 2:

                        @pl.when(is_hub)
                        def _():
                            mix_copy(c, b, 0).wait_send()


def hand_over(a, b, a_out, b_out, sem):
    copies = [pltpu.make_async_copy(a, a_out, sem.at[0]), pltpu.make_async_copy(b, b_out, sem.at[1])]
    for copy in copies:
        copy.start()
    for copy in copies:
        copy.wait()


def on_device(
    n_dp,
    n_mp,
    section_rows,
    proj_weights,
    out_grad,
    ffn_gain,
    ffn_in,
    ffn_out,
    grow_level,
    dec_seg,
    enc_seg,
):
    rows = section_rows[0]
    n_rows, width = rows.shape
    heads, lanes = proj_weights.shape[2:]
    weight = proj_weights.reshape(width * heads, lanes)
    units = ffn_out.shape[0]
    gates = jnp.transpose(ffn_in, (1, 2, 0)).reshape(2 * units, width)
    block, share, cut = width // n_mp, width // (2 * n_mp), width // n_dp
    relays = math.gcd(n_dp, most_relays)
    vmem = pl.BlockSpec(memory_space=pltpu.VMEM)

    def sems(*shape):
        return pltpu.SemaphoreType.DMA(shape)

    operands = (
        rows,
        weight,
        out_grad,
        ffn_gain[None],
        gates,
        ffn_out,
        grow_level[None],
        dec_seg,
        enc_seg,
    )
    layer_out, grads = pl.pallas_call(
        functools.partial(body, n_dp, n_mp),
        out_shape=(
            pltpu.VMEM((n_rows, share), BF16),
            pltpu.VMEM((cut * heads, lanes), BF16),
        ),
        in_specs=[pl.BlockSpec(memory_space=pltpu.MemorySpace.HBM)] * 9,
        out_specs=(vmem, vmem),
        scratch_shapes=[pltpu.VMEM(a.shape, a.dtype) for a in operands if a is not ffn_out]
        + [
            pltpu.VMEM((units, width // 2), BF16),
            pltpu.VMEM((units, width // 2), BF16),
            pltpu.VMEM((width, lanes), BF16),
            pltpu.VMEM((width, lanes), BF16),
            pltpu.VMEM((2, n_rows, lanes), BF16),
            pltpu.VMEM((2, n_rows, lanes), BF16),
            pltpu.VMEM((block, n_mp * lanes), BF16),
            pltpu.VMEM((n_rows, n_mp * lanes), BF16),
            pltpu.VMEM((n_dp, n_rows, cut), BF16),
            pltpu.VMEM((n_dp, n_rows, cut), BF16),
            pltpu.VMEM((n_rows, 2 * lanes), BF16),
            pltpu.VMEM((n_dp, n_rows, 2 * lanes), BF16),
            pltpu.VMEM((n_mp, n_rows, block), BF16),
            pltpu.VMEM((n_rows, 2 * units), F32),
            pltpu.VMEM((n_rows, lanes), F32),
            pltpu.VMEM((n_rows, units), BF16),
            pltpu.VMEM((n_rows, units), BF16),
            pltpu.VMEM((n_mp, n_rows, share), F32),
            pltpu.VMEM((n_mp, n_rows, share), BF16),
            pltpu.VMEM((n_mp, n_rows, share), BF16),
            pltpu.VMEM((lanes, cut), BF16),
            pltpu.VMEM((lanes, cut), BF16),
            sems(2, n_dp - 1),
            sems(2, n_dp - 1),
            sems(2, n_dp - 1),
            sems(2, n_mp - 1),
            sems(2, n_mp - 1, max(relays - 1, 1)),
            sems(2, n_mp),
            sems(n_mp - 1, pieces),
            sems(pieces, n_mp),
            sems(2, pieces, n_mp),
            sems(2, pieces),
            sems(pieces, n_mp),
            sems(pieces, n_mp),
            sems(2),
            sems(2),
            sems(2),
            sems(n_mp),
            sems(8),
            sems(2),
        ],
        compiler_params=pltpu.CompilerParams(
            collective_id=0, has_side_effects=True, vmem_limit_bytes=58 << 20
        ),
    )(*operands)
    layer_out, grads = pl.pallas_call(
        hand_over,
        out_shape=(
            jax.ShapeDtypeStruct(layer_out.shape, BF16),
            jax.ShapeDtypeStruct(grads.shape, BF16),
        ),
        in_specs=[vmem] * 2,
        out_specs=(pl.BlockSpec(memory_space=pl.ANY),) * 2,
        scratch_shapes=[pltpu.SemaphoreType.DMA((2,))],
    )(*(pltpu.with_memory_space_constraint(a, pltpu.VMEM) for a in (layer_out, grads)))
    return (layer_out, grads.reshape(1, cut, heads, lanes))


def solution(mesh):
    in_specs = (
        P("sec", "dp", None),
        P("sec", None, "mp", None),
        P("dp", None),
        P(),
        P(None, None, ("sec", "mp")),
        P(("sec", "mp"), None),
        P(("sec", "mp")),
        P("dp", None),
        P("dp", None),
    )
    out_specs = (P("dp", ("sec", "mp")), P("sec", "dp", "mp", None))
    return jax.shard_map(
        functools.partial(on_device, mesh.shape["dp"], mesh.shape["mp"]),
        mesh=mesh,
        in_specs=in_specs,
        out_specs=out_specs,
        check_vma=False,
    )
```

```python
import functools
import math

import jax
import jax.numpy as jnp
from jax import lax
from jax.experimental import pallas as pl
from jax.experimental.pallas import tpu as pltpu
from jax.sharding import PartitionSpec as P

norm_eps = 1e-06
eighths = (4, 4)
pieces = len(eighths)
most_relays = 4
F32 = jnp.float32
BF16 = jnp.bfloat16


def contract(left, right, left_dim, right_dim):
    dims = (((left_dim,), (right_dim,)), ((), ()))
    return lax.dot_general(left, right, dims, preferred_element_type=F32)


def remote(src, dst, send, recv, device):
    return pltpu.make_async_remote_copy(
        src_ref=src,
        dst_ref=dst,
        send_sem=send,
        recv_sem=recv,
        device_id=device,
        device_id_type=pl.DeviceIdType.MESH,
    )


def body(
    n_dp,
    n_mp,
    rows_hbm,
    weight_hbm,
    grad_hbm,
    gain_hbm,
    ffn_in_hbm,
    ffn_out_hbm,
    level_hbm,
    dec_seg_hbm,
    enc_seg_hbm,
    layer_out,
    proj_grads,
    rows,
    weight,
    grad,
    gain,
    ffn_in,
    level,
    dec_seg,
    enc_seg,
    down_own,
    down_other,
    w_left,
    w_right,
    kv_send,
    kv_recv,
    wo_all,
    ctx_all,
    rows_all,
    grad_all,
    g_send,
    g_all,
    mix,
    gate_up,
    square,
    hid_own,
    hid_other,
    partial,
    fold_send,
    fold_recv,
    t_left,
    t_right,
    rows_sem,
    grad_sem,
    g_sem,
    wo_sem,
    relay_sem,
    ctx_sem,
    mix_send,
    mix_recv,
    fwd_sent,
    fwd_sem,
    hid_sem,
    fold_sem,
    fold_got,
    kv_sem,
    gkv_sem,
    down_sem,
    weight_sem,
    load_sem,
    slot_sem,
):
    sec = lax.axis_index("sec")
    dp = lax.axis_index("dp")
    mp = lax.axis_index("mp")
    n_rows, width = rows.shape
    lanes = weight.shape[1]
    half = lanes // 2
    block = width // n_mp
    share = width // (2 * n_mp)
    cut = width // n_dp
    units = down_own.shape[0]
    hubs = n_mp == 4
    if hubs:
        hub = mp * (3 - mp) // 2
        mate = mp + 1 - 2 * lax.rem(mp, 2)
        far_hub = 3 - mp * hub - mate * (1 - hub)
        far_end = 3 - mate * hub - mp * (1 - hub)
        is_hub = hub == 1
    if hubs:
        arrivals = [mate, far_hub, far_end]
    else:
        arrivals = [lax.rem(mp + n_mp - t, n_mp) for t in range(1, n_mp)]
    if n_mp == 4:
        targets = [far_end, far_hub, mate]
        sequence = [mate, far_hub, far_end]
    else:
        targets = [lax.rem(mp + t, n_mp) for t in range(1, n_mp)]
        sequence = [lax.rem(mp + n_mp - t, n_mp) for t in range(1, n_mp)]
    starts = [sum(eighths[:c]) * n_rows // 8 for c in range(pieces + 1)]
    relays = math.gcd(n_dp, most_relays)
    part = block // relays
    turn = lax.rem(dp, relays)
    is_dec = sec == 1
    is_enc = sec == 0
    other = {"sec": 1 - sec}

    def dp_at(t):
        return lax.rem(dp + t, n_dp)

    def mp_at(t):
        return lax.rem(mp + t, n_mp)

    def turn_at(s):
        return lax.rem(turn + s, relays)

    def cols(index, size):
        return pl.ds(pl.multiple_of(index * size, size), size)

    def piece(c):
        return pl.ds(starts[c], starts[c + 1] - starts[c])

    def signal(device):
        pl.semaphore_signal(barrier, inc=1, device_id=device, device_id_type=pl.DeviceIdType.MESH)

    def weight_load(t):
        where = cols(mp_at(t), 2 * block)
        return pltpu.make_async_copy(
            weight_hbm.at[where, :], weight.at[where, :], weight_sem.at[t]
        )

    pairs = (
        (rows_hbm, rows),
        (grad_hbm, grad),
        (dec_seg_hbm, dec_seg),
        (enc_seg_hbm, enc_seg),
        (gain_hbm, gain),
        (level_hbm, level),
        (ffn_in_hbm, ffn_in),
        (ffn_out_hbm.at[:, cols(sec, width // 2)], down_own),
    )
    loads = [pltpu.make_async_copy(a, b, load_sem.at[i]) for i, (a, b) in enumerate(pairs)]
    own_rows = pltpu.make_async_copy(rows_hbm.at[:, cols(dp, cut)], rows_all.at[0], slot_sem.at[0])
    own_grad = pltpu.make_async_copy(grad_hbm.at[:, cols(dp, cut)], grad_all.at[0], slot_sem.at[1])

    def rows_copy(t):
        to = dp_at(t)
        return remote(
            rows_hbm.at[:, cols(to, cut)], rows_all.at[t], rows_sem.at[0], rows_sem.at[1], {"dp": to}
        )

    def grad_copy(t):
        to = dp_at(t)
        return remote(
            grad_hbm.at[:, cols(to, cut)], grad_all.at[t], grad_sem.at[0], grad_sem.at[1], {"dp": to}
        )

    def g_copy(t):
        return remote(
            g_all.at[0], g_all.at[t], g_sem.at[0], g_sem.at[1], {"dp": dp_at(t)}
        )

    def whole_of(ref, sem):
        return remote(ref, ref, sem.at[0], sem.at[1], other)

    peers = pl.ds(1, n_dp - 1)
    rows_total = whole_of(rows_all.at[peers], rows_sem)
    grad_total = whole_of(grad_all.at[peers], grad_sem)
    g_total = whole_of(g_all.at[peers], g_sem)
    ctx_total = whole_of(ctx_all.at[:, lanes:], ctx_sem)

    def relay_total(t):
        ref = wo_all.at[pl.ds(0, (relays - 1) * part), slot(t)]
        return remote(ref, ref, relay_sem.at[0, t - 1], relay_sem.at[1, t - 1], other)

    def mix_total(c, count, sem):
        ref = mix.at[pl.ds(0, count), piece(c), :]
        return remote(ref, ref, sem.at[c], mix_recv.at[c, 0], other)

    def fold_total(c):
        ref = fold_send.at[pl.ds(0, n_mp - 1), piece(c), :]
        return remote(ref, ref, fold_sem.at[c], fold_got.at[c, 0], other)

    def slot(t):
        return slice(t * lanes, (t + 1) * lanes)

    def adjacent(t, sending):
        if t == 1:
            return mp < n_mp - 1 if sending else mp > 0
        return mp > 0 if sending else mp < n_mp - 1

    def near_far(t, sending, near, far):
        if 1 < t < n_mp - 1:
            far()
        else:
            pl.when(adjacent(t, sending))(near)
            pl.when(jnp.logical_not(adjacent(t, sending)))(far)

    def wo_copy(t):
        to = mp_at(t)
        return remote(
            w_right.at[cols(to * relays + turn, part), :],
            wo_all.at[cols(turn, part), slot(t)],
            wo_sem.at[0, t - 1],
            wo_sem.at[1, t - 1],
            {"mp": to},
        )

    def wo_whole(t):
        to = mp_at(t)
        return remote(
            w_right.at[cols(to, block), :],
            wo_all.at[:, slot(t)],
            wo_sem.at[0, t - 1],
            wo_sem.at[1, t - 1],
            {"mp": to},
        )

    def relay_out(t, s):
        ref = wo_all.at[cols(turn, part), slot(t)]
        to = {"dp": dp - turn + turn_at(s)}
        return remote(ref, ref, relay_sem.at[0, t - 1], relay_sem.at[1, t - 1], to)

    def relay_in(t, s):
        ref = wo_all.at[cols(turn_at(relays - s), part), slot(t)]
        to = {"dp": dp - turn + turn_at(s)}
        return remote(ref, ref, relay_sem.at[0, t - 1], relay_sem.at[1, t - 1], to)

    def ctx_copy(t):
        return remote(
            ctx_all.at[:, slot(0)],
            ctx_all.at[:, slot(t)],
            ctx_sem.at[0],
            ctx_sem.at[1],
            {"mp": mp_at(t)},
        )

    def mix_copy(c, b, j):
        ref = mix.at[b, piece(c), :]
        return remote(ref, ref, mix_send.at[c], mix_recv.at[c, b], {"mp": targets[j]})

    def fwd_copy(c, b):
        ref = mix.at[b, piece(c), :]
        return remote(ref, ref, fwd_sent.at[c], fwd_sem.at[c, b], other)

    def hid_copy(c):
        return remote(
            hid_own.at[piece(c), :], hid_other.at[piece(c), :], hid_sem.at[0, c], hid_sem.at[1, c], other
        )

    def fold_copy(c, k):
        if hubs:
            into = 1 + (1 - hub) * k if k else 0
            to = hub * arrivals[k] + (1 - hub) * mate
        else:
            into, to = k, arrivals[k]
        return remote(
            fold_send.at[k, piece(c), :],
            fold_recv.at[into, piece(c), :],
            fold_sem.at[c],
            fold_got.at[c, into],
            {"mp": to},
        )

    def fold_in(c, k):
        return remote(
            fold_send.at[0, piece(c), :],
            fold_recv.at[k, piece(c), :],
            fold_sem.at[c],
            fold_got.at[c, k],
            {"mp": arrivals[0]},
        )

    def send_own(c):
        for j in range(len(targets)):
            mix_copy(c, mp, j).start()

    kv_copy = remote(kv_send, kv_recv, kv_sem.at[0], kv_sem.at[1], other)
    gkv_copy = remote(g_send, g_all.at[0], gkv_sem.at[0], gkv_sem.at[1], other)
    down_copy = remote(
        ffn_out_hbm.at[:, cols(1 - sec, width // 2)], down_other, down_sem.at[0], down_sem.at[1], other
    )

    order = list(range(2, n_mp - 1)) + [1, n_mp - 1, 0]
    if n_dp == 4:
        beside = 1 + 2 * lax.rem(dp, 2)
        near_dp, far_dp = [beside, 2], [4 - beside]
    else:
        near_dp, far_dp = [1], list(range(2, n_dp))
    with jax.named_scope("signals"):
        barrier = pltpu.get_barrier_semaphore()
        for t in order:
            weight_load(t).start()
        for load in loads[:1]:
            load.start()
        signal(other)
        for t in range(1, n_dp):
            signal({"dp": dp_at(t)})
        for t in range(1, n_mp):
            signal({"mp": mp_at(t)})

    tile = 2 * lanes
    out_id = lax.broadcasted_iota(jnp.int32, (tile, tile), 0)
    in_id = lax.broadcasted_iota(jnp.int32, (tile, tile), 1)
    wanted = jnp.where(out_id < lanes, 2 * out_id, 2 * (out_id - lanes) + 1)
    pick = jnp.where(in_id == wanted, 1.0, 0.0).astype(BF16)
    first = lax.broadcasted_iota(jnp.int32, (lanes, lanes), 1) < half

    for t in order:
        with jax.named_scope("split%d" % t):
            begin = mp_at(t) * block
            weight_load(t).wait()
            for i in range(block // lanes):
                d = pl.multiple_of(begin + i * lanes, lanes)
                two = contract(pick, weight[pl.ds(pl.multiple_of(2 * d, tile), tile), :], 1, 0)
                one, second = two[:lanes], two[lanes:]
                w_left[pl.ds(d, lanes), :] = jnp.where(
                    first, one, pltpu.roll(second, half, 1)
                ).astype(BF16)
                w_right[pl.ds(d, lanes), :] = jnp.where(
                    first, pltpu.roll(one, half, 1), second
                ).astype(BF16)
        if t == order[0]:
            for load in loads[1:6]:
                load.start()
            with jax.named_scope("barrier"):
                pl.semaphore_wait(barrier, n_dp + n_mp - 1)

            @pl.when(is_enc)
            def _():
                for t in near_dp:
                    rows_copy(t).start()

        if t > 0:

            @pl.when(is_dec)
            def _():
                near_far(t, True, lambda: None, lambda: wo_copy(t).start())

    loads[0].wait()

    @pl.when(is_enc)
    def _():
        with jax.named_scope("kv"):
            kv_send[0] = contract(rows[...], w_left[...], 1, 0).astype(BF16)
            kv_send[1] = contract(rows[...], w_right[...], 1, 0).astype(BF16)
            kv_copy.start()

    for load in loads[6:]:
        load.start()
    own_rows.start()
    down_copy.start()
    for load in loads[1:6]:
        load.wait()

    @pl.when(is_dec)
    def _():
        own_grad.start()
        for t in (1, n_mp - 1):
            near_far(t, True, lambda: wo_whole(t).start(), lambda: None)
        with jax.named_scope("q_gc"):
            wide_q = contract(rows[...], w_left[...], 1, 0)
            wide_gc = contract(grad[...], w_right[...], 1, 0)
            q = wide_q.astype(BF16)
            gc = wide_gc.astype(BF16)
            dec = jnp.transpose(jnp.broadcast_to(dec_seg[...].astype(F32), (n_rows, n_rows)))
            same = dec == jnp.broadcast_to(enc_seg[...].astype(F32), (n_rows, n_rows))
            wo_all[:, slot(0)] = w_right[cols(mp, block), :]
        with jax.named_scope("relay"):
            for t in order[:-1]:

                def pass_quarter():
                    wo_copy(t).wait_recv()
                    for s in range(1, relays):
                        relay_out(t, s).start()

                near_far(t, False, lambda: None, pass_quarter)
        with jax.named_scope("kv_wait"):
            kv_copy.wait_recv()
        with jax.named_scope("attend"):
            key = kv_recv[0]
            value = kv_recv[1]
            probs, lows, contexts = [], [], []
            for h in range(2):
                mine = first if h == 0 else jnp.logical_not(first)
                scores = contract(jnp.where(mine, wide_q, 0.0).astype(BF16), key, 1, 1)
                scores = jnp.where(same, scores, -1e30)
                scores = jnp.exp(scores - jnp.max(scores, axis=1, keepdims=True))
                prob = scores / jnp.sum(scores, axis=1, keepdims=True)
                low = prob.astype(BF16)
                probs.append(prob)
                lows.append(low)
                contexts.append(contract(low, value, 1, 0))
            context = jnp.where(first, contexts[0], contexts[1]).astype(BF16)
            ctx_all[:, slot(0)] = context
            g_all[0, :, lanes:] = context
            for t in range(1, n_mp):
                ctx_copy(t).start()
        with jax.named_scope("attend_back"):
            gqs, gks, gvs = [], [], []
            for h in range(2):
                mine = first if h == 0 else jnp.logical_not(first)
                grad_prob = contract(jnp.where(mine, wide_gc, 0.0).astype(BF16), value, 1, 1)
                total = jnp.sum(grad_prob * probs[h], axis=1, keepdims=True)
                score = (probs[h] * (grad_prob - total)).astype(BF16)
                gqs.append(contract(score, key, 1, 0))
                gks.append(contract(score, q, 0, 0))
                gvs.append(contract(lows[h], gc, 0, 0))
            g_send[:, :lanes] = jnp.where(first, gks[0], gks[1]).astype(BF16)
            g_send[:, lanes:] = jnp.where(first, gvs[0], gvs[1]).astype(BF16)
            gkv_copy.start()
            g_all[0, :, :lanes] = jnp.where(first, gqs[0], gqs[1]).astype(BF16)

    @pl.when(is_enc)
    def _():
        with jax.named_scope("gkv_wait"):
            gkv_copy.wait_recv()
            for t in far_dp:
                rows_copy(t).start()

    @pl.when(is_dec)
    def _():
        with jax.named_scope("wo_wait"):
            for t in range(1, n_mp):

                def take_quarters():
                    if relays > 1:
                        relay_total(t).wait_recv()

                near_far(t, False, lambda: wo_whole(t).wait_recv(), take_quarters)
        for t in range(1, n_dp):
            rows_copy(t).start()
            grad_copy(t).start()
            g_copy(t).start()
        with jax.named_scope("ctx_wait"):
            ctx_total.wait_recv()
        with jax.named_scope("mix"):
            for c in range(pieces):
                own = contract(ctx_all[piece(c), :], wo_all[...], 1, 1)
                total = rows[piece(c), cols(mp, block)].astype(F32) + own
                mix[mp, piece(c), :] = total.astype(BF16)

                send_own(c)
                fwd_copy(c, mp).start()

    for load in loads[6:]:
        load.wait()

    def take(c, b, fresh):
        where = cols(b, block)
        wide = mix[b, piece(c), :].astype(F32)
        scaled = (wide * gain[:, where]).astype(BF16)
        both = contract(scaled, ffn_in[:, where], 1, 1)
        squares = jnp.sum(wide * wide, axis=1, keepdims=True)
        squares = jnp.broadcast_to(squares, (wide.shape[0], lanes))
        if fresh:
            gate_up[piece(c), :] = both
            square[piece(c), :] = squares
        else:
            gate_up[piece(c), :] += both
            square[piece(c), :] += squares

    place = sec * n_mp + mp
    def gather(c):
        @pl.when(is_enc)
        def _():
            fwd_copy(c, mp).wait_recv()
            if c == 0:
                for t in range(1, n_dp):
                    g_copy(t).start()

        take(c, mp, True)
        for k, b in enumerate(sequence):

            @pl.when(is_dec)
            def _():
                mix_copy(c, b, 0).wait_recv()
                fwd_copy(c, b).start()

            @pl.when(is_enc)
            def _():
                fwd_copy(c, b).wait_recv()

            take(c, b, False)

    def activate(c):
        with jax.named_scope("hidden%d" % c):
            inverse = lax.rsqrt(square[piece(c), :1] / width + norm_eps)
            gate = gate_up[piece(c), :units] * inverse
            up = gate_up[piece(c), units:] * inverse
            unit_level = level[...].astype(F32) * 0.25
            hidden = (jax.nn.gelu(gate, approximate=True) * up * unit_level).astype(BF16)
            hid_own[piece(c), :] = hidden
            hid_copy(c).start()

    def descend(c):
        with jax.named_scope("down_own%d" % c):
            hidden = hid_own[piece(c), :]
            for k in reversed(range(n_mp - 1)):
                partial[k, piece(c), :] = contract(hidden, down_own[:, cols(arrivals[k], share)], 1, 0)
        if c > 0:
            with jax.named_scope("combine%d" % (c - 1)):
                combine(c - 1)
        with jax.named_scope("hid_wait%d" % c):
            if c == 0:
                down_copy.wait_recv()
            hid_copy(c).wait_recv()
        with jax.named_scope("down%d" % c):
            beside_hidden = hid_other[piece(c), :]

            def product(b):
                where = cols(b, share)
                own = contract(hidden, down_own[:, where], 1, 0)
                return own + contract(beside_hidden, down_other[:, where], 1, 0)

            for k in reversed(range(n_mp - 1)):
                other_part = contract(beside_hidden, down_other[:, cols(arrivals[k], share)], 1, 0)
                own = partial[k, piece(c), :] + other_part
                fold_send[k, piece(c), :] = own.astype(BF16)
                if not hubs or k == 0:
                    fold_copy(c, k).start()
                else:
                    partial[k, piece(c), :] = own

                    @pl.when(jnp.logical_not(is_hub))
                    def _():
                        fold_copy(c, k).start()

            there = cols(lax.rem(place, 2), share)
            partial[0, piece(c), :] = product(mp) + mix[place // 2, piece(c), there].astype(F32)

    def combine(c):
        if hubs:

            @pl.when(is_hub)
            def _():
                for k in range(n_mp - 2, 0, -1):
                    fold_in(c, k + 1).wait_recv()
                    total = partial[k, piece(c), :] + fold_recv[k + 1, piece(c), :].astype(F32)
                    fold_send[k, piece(c), :] = total.astype(BF16)
                    fold_copy(c, k).start()

    for c in range(pieces):
        with jax.named_scope("gather%d" % c):
            gather(c)
        activate(c)
        descend(c)
    with jax.named_scope("combine%d" % (pieces - 1)):
        combine(pieces - 1)

    own_rows.wait()

    @pl.when(is_dec)
    def _():
        own_grad.wait()

    with jax.named_scope("dp_wait"):
        rows_total.wait_recv()
        g_total.wait_recv()

        @pl.when(is_dec)
        def _():
            grad_total.wait_recv()

    with jax.named_scope("weight_grads"):
        flat_rows = rows_all[...].reshape(n_dp * n_rows, cut)
        g_flat = g_all[...].reshape(n_dp * n_rows, 2 * lanes)
        t_left[...] = contract(g_flat[:, :lanes], flat_rows, 0, 0).astype(BF16)

        @pl.when(is_enc)
        def _():
            t_right[...] = contract(g_flat[:, lanes:], flat_rows, 0, 0).astype(BF16)

        @pl.when(is_dec)
        def _():
            flat_grad = grad_all[...].reshape(n_dp * n_rows, cut)
            t_right[...] = contract(g_flat[:, lanes:], flat_grad, 0, 0).astype(BF16)

        row_id = lax.broadcasted_iota(jnp.int32, (tile, lanes), 0)
        d_id = lax.broadcasted_iota(jnp.int32, (tile, lanes), 1)
        spread = [jnp.where(row_id == 2 * d_id + h, 1.0, 0.0).astype(BF16) for h in range(2)]
        for i in range(cut // lanes):
            some = slice(i * lanes, (i + 1) * lanes)
            heads = [
                jnp.concatenate(
                    [t_left[h * half : (h + 1) * half, some], t_right[h * half : (h + 1) * half, some]],
                    axis=0,
                )
                for h in range(2)
            ]
            woven = contract(spread[0], heads[0], 1, 1) + contract(spread[1], heads[1], 1, 1)
            proj_grads[i * tile : (i + 1) * tile, :] = woven.astype(BF16)

    with jax.named_scope("fold"):
        for c in range(pieces):
            mine = partial[0, piece(c), :]
            for k in range(2 if hubs else n_mp - 1):
                fold_in(c, k).wait_recv()
                mine = mine + fold_recv[k, piece(c), :].astype(F32)
            layer_out[piece(c), :] = mine.astype(BF16)

    with jax.named_scope("drain"):
        down_copy.wait_send()
        rows_total.wait_send()
        g_total.wait_send()
        for c in range(pieces):
            hid_copy(c).wait_send()
            fold_total(c).wait_send()

        @pl.when(is_enc)
        def _():
            kv_copy.wait_send()

        @pl.when(is_dec)
        def _():
            gkv_copy.wait_send()
            grad_total.wait_send()
            ctx_total.wait_send()
            for t in range(1, n_mp):
                near_far(t, True, lambda: wo_whole(t).wait_send(), lambda: wo_copy(t).wait_send())
                if relays > 1:
                    near_far(t, False, lambda: None, lambda: relay_total(t).wait_send())
            for c in range(pieces):
                mix_total(c, n_mp, fwd_sent).wait_send()
                mix_total(c, n_mp - 1, mix_send).wait_send()


def hand_over(a, b, a_out, b_out, sem):
    copies = [pltpu.make_async_copy(a, a_out, sem.at[0]), pltpu.make_async_copy(b, b_out, sem.at[1])]
    for copy in copies:
        copy.start()
    for copy in copies:
        copy.wait()


def on_device(
    n_dp,
    n_mp,
    section_rows,
    proj_weights,
    out_grad,
    ffn_gain,
    ffn_in,
    ffn_out,
    grow_level,
    dec_seg,
    enc_seg,
):
    rows = section_rows[0]
    n_rows, width = rows.shape
    heads, lanes = proj_weights.shape[2:]
    weight = proj_weights.reshape(width * heads, lanes)
    units = ffn_out.shape[0]
    gates = jnp.transpose(ffn_in, (1, 2, 0)).reshape(2 * units, width)
    block, share, cut = width // n_mp, width // (2 * n_mp), width // n_dp
    relays = math.gcd(n_dp, most_relays)
    vmem = pl.BlockSpec(memory_space=pltpu.VMEM)

    def sems(*shape):
        return pltpu.SemaphoreType.DMA(shape)

    operands = (
        rows,
        weight,
        out_grad,
        ffn_gain[None],
        gates,
        ffn_out,
        grow_level[None],
        dec_seg,
        enc_seg,
    )
    layer_out, grads = pl.pallas_call(
        functools.partial(body, n_dp, n_mp),
        out_shape=(
            pltpu.VMEM((n_rows, share), BF16),
            pltpu.VMEM((cut * heads, lanes), BF16),
        ),
        in_specs=[pl.BlockSpec(memory_space=pltpu.MemorySpace.HBM)] * 9,
        out_specs=(vmem, vmem),
        scratch_shapes=[pltpu.VMEM(a.shape, a.dtype) for a in operands if a is not ffn_out]
        + [
            pltpu.VMEM((units, width // 2), BF16),
            pltpu.VMEM((units, width // 2), BF16),
            pltpu.VMEM((width, lanes), BF16),
            pltpu.VMEM((width, lanes), BF16),
            pltpu.VMEM((2, n_rows, lanes), BF16),
            pltpu.VMEM((2, n_rows, lanes), BF16),
            pltpu.VMEM((block, n_mp * lanes), BF16),
            pltpu.VMEM((n_rows, n_mp * lanes), BF16),
            pltpu.VMEM((n_dp, n_rows, cut), BF16),
            pltpu.VMEM((n_dp, n_rows, cut), BF16),
            pltpu.VMEM((n_rows, 2 * lanes), BF16),
            pltpu.VMEM((n_dp, n_rows, 2 * lanes), BF16),
            pltpu.VMEM((n_mp, n_rows, block), BF16),
            pltpu.VMEM((n_rows, 2 * units), F32),
            pltpu.VMEM((n_rows, lanes), F32),
            pltpu.VMEM((n_rows, units), BF16),
            pltpu.VMEM((n_rows, units), BF16),
            pltpu.VMEM((n_mp, n_rows, share), F32),
            pltpu.VMEM((n_mp, n_rows, share), BF16),
            pltpu.VMEM((n_mp, n_rows, share), BF16),
            pltpu.VMEM((lanes, cut), BF16),
            pltpu.VMEM((lanes, cut), BF16),
            sems(2),
            sems(2),
            sems(2),
            sems(2, n_mp - 1),
            sems(2, n_mp - 1),
            sems(2),
            sems(pieces),
            sems(pieces, n_mp),
            sems(pieces),
            sems(pieces, n_mp),
            sems(2, pieces),
            sems(pieces),
            sems(pieces, n_mp),
            sems(2),
            sems(2),
            sems(2),
            sems(n_mp),
            sems(8),
            sems(2),
        ],
        compiler_params=pltpu.CompilerParams(
            collective_id=0, has_side_effects=True, vmem_limit_bytes=58 << 20
        ),
    )(*operands)
    layer_out, grads = pl.pallas_call(
        hand_over,
        out_shape=(
            jax.ShapeDtypeStruct(layer_out.shape, BF16),
            jax.ShapeDtypeStruct(grads.shape, BF16),
        ),
        in_specs=[vmem] * 2,
        out_specs=(pl.BlockSpec(memory_space=pl.ANY),) * 2,
        scratch_shapes=[pltpu.SemaphoreType.DMA((2,))],
    )(*(pltpu.with_memory_space_constraint(a, pltpu.VMEM) for a in (layer_out, grads)))
    return (layer_out, grads.reshape(1, cut, heads, lanes))


def solution(mesh):
    in_specs = (
        P("sec", "dp", None),
        P("sec", None, "mp", None),
        P("dp", None),
        P(),
        P(None, None, ("sec", "mp")),
        P(("sec", "mp"), None),
        P(("sec", "mp")),
        P("dp", None),
        P("dp", None),
    )
    out_specs = (P("dp", ("sec", "mp")), P("sec", "dp", "mp", None))
    return jax.shard_map(
        functools.partial(on_device, mesh.shape["dp"], mesh.shape["mp"]),
        mesh=mesh,
        in_specs=in_specs,
        out_specs=out_specs,
        check_vma=False,
    )
```

```python
import functools
import math

import jax
import jax.numpy as jnp
from jax import lax
from jax.experimental import pallas as pl
from jax.experimental.pallas import tpu as pltpu
from jax.sharding import PartitionSpec as P

norm_eps = 1e-06
eighths = (4, 4)
pieces = len(eighths)
most_relays = 4
F32 = jnp.float32
BF16 = jnp.bfloat16


def contract(left, right, left_dim, right_dim):
    dims = (((left_dim,), (right_dim,)), ((), ()))
    return lax.dot_general(left, right, dims, preferred_element_type=F32)


def remote(src, dst, send, recv, device):
    return pltpu.make_async_remote_copy(
        src_ref=src,
        dst_ref=dst,
        send_sem=send,
        recv_sem=recv,
        device_id=device,
        device_id_type=pl.DeviceIdType.MESH,
    )


def body(
    n_dp,
    n_mp,
    rows_hbm,
    weight_hbm,
    grad_hbm,
    gain_hbm,
    ffn_in_hbm,
    ffn_out_hbm,
    level_hbm,
    dec_seg_hbm,
    enc_seg_hbm,
    layer_out,
    proj_grads,
    rows,
    weight,
    grad,
    gain,
    ffn_in,
    level,
    dec_seg,
    enc_seg,
    down_own,
    down_other,
    w_left,
    w_right,
    kv_send,
    kv_recv,
    wo_all,
    ctx_all,
    rows_all,
    grad_all,
    g_send,
    g_all,
    mix,
    gate_up,
    square,
    hid_own,
    hid_other,
    partial,
    fold_send,
    fold_recv,
    t_left,
    t_right,
    rows_sem,
    grad_sem,
    g_sem,
    wo_sem,
    relay_sem,
    ctx_sem,
    mix_send,
    mix_recv,
    fwd_sent,
    fwd_sem,
    hid_sem,
    fold_sem,
    fold_got,
    kv_sem,
    gkv_sem,
    down_sem,
    weight_sem,
    load_sem,
    slot_sem,
):
    sec = lax.axis_index("sec")
    dp = lax.axis_index("dp")
    mp = lax.axis_index("mp")
    n_rows, width = rows.shape
    lanes = weight.shape[1]
    half = lanes // 2
    block = width // n_mp
    share = width // (2 * n_mp)
    cut = width // n_dp
    units = down_own.shape[0]
    hubs = n_mp == 4
    if hubs:
        hub = mp * (3 - mp) // 2
        mate = mp + 1 - 2 * lax.rem(mp, 2)
        far_hub = 3 - mp * hub - mate * (1 - hub)
        far_end = 3 - mate * hub - mp * (1 - hub)
        is_hub = hub == 1
    if hubs:
        arrivals = [mate, far_hub, far_end]
    else:
        arrivals = [lax.rem(mp + n_mp - t, n_mp) for t in range(1, n_mp)]
    if n_mp == 4:
        targets = [far_end, mate, far_hub]
        sequence = [mate, far_hub, far_end]
    else:
        targets = [lax.rem(mp + t, n_mp) for t in range(1, n_mp)]
        sequence = [lax.rem(mp + n_mp - t, n_mp) for t in range(1, n_mp)]
    starts = [sum(eighths[:c]) * n_rows // 8 for c in range(pieces + 1)]
    relays = math.gcd(n_dp, most_relays)
    part = block // relays
    turn = lax.rem(dp, relays)
    is_dec = sec == 1
    is_enc = sec == 0
    other = {"sec": 1 - sec}

    def dp_at(t):
        return lax.rem(dp + t, n_dp)

    def mp_at(t):
        return lax.rem(mp + t, n_mp)

    def turn_at(s):
        return lax.rem(turn + s, relays)

    def cols(index, size):
        return pl.ds(pl.multiple_of(index * size, size), size)

    def piece(c):
        return pl.ds(starts[c], starts[c + 1] - starts[c])

    def signal(device):
        pl.semaphore_signal(barrier, inc=1, device_id=device, device_id_type=pl.DeviceIdType.MESH)

    def weight_load(t):
        where = cols(mp_at(t), 2 * block)
        return pltpu.make_async_copy(
            weight_hbm.at[where, :], weight.at[where, :], weight_sem.at[t]
        )

    pairs = (
        (rows_hbm, rows),
        (grad_hbm, grad),
        (dec_seg_hbm, dec_seg),
        (enc_seg_hbm, enc_seg),
        (gain_hbm, gain),
        (level_hbm, level),
        (ffn_in_hbm, ffn_in),
        (ffn_out_hbm.at[:, cols(sec, width // 2)], down_own),
    )
    loads = [pltpu.make_async_copy(a, b, load_sem.at[i]) for i, (a, b) in enumerate(pairs)]
    own_rows = pltpu.make_async_copy(rows_hbm.at[:, cols(dp, cut)], rows_all.at[0], slot_sem.at[0])
    own_grad = pltpu.make_async_copy(grad_hbm.at[:, cols(dp, cut)], grad_all.at[0], slot_sem.at[1])

    def rows_copy(t):
        to = dp_at(t)
        return remote(
            rows_hbm.at[:, cols(to, cut)], rows_all.at[t], rows_sem.at[0], rows_sem.at[1], {"dp": to}
        )

    def grad_copy(t):
        to = dp_at(t)
        return remote(
            grad_hbm.at[:, cols(to, cut)], grad_all.at[t], grad_sem.at[0], grad_sem.at[1], {"dp": to}
        )

    def g_copy(t):
        return remote(
            g_all.at[0], g_all.at[t], g_sem.at[0], g_sem.at[1], {"dp": dp_at(t)}
        )

    def whole_of(ref, sem):
        return remote(ref, ref, sem.at[0], sem.at[1], other)

    peers = pl.ds(1, n_dp - 1)
    rows_total = whole_of(rows_all.at[peers], rows_sem)
    grad_total = whole_of(grad_all.at[peers], grad_sem)
    g_total = whole_of(g_all.at[peers], g_sem)
    ctx_total = whole_of(ctx_all.at[:, lanes:], ctx_sem)

    def relay_total(t):
        ref = wo_all.at[pl.ds(0, (relays - 1) * part), slot(t)]
        return remote(ref, ref, relay_sem.at[0, t - 1], relay_sem.at[1, t - 1], other)

    def mix_total(c, count, sem):
        ref = mix.at[pl.ds(0, count), piece(c), :]
        return remote(ref, ref, sem.at[c], mix_recv.at[c, 0], other)

    def fold_total(c):
        ref = fold_send.at[pl.ds(0, n_mp - 1), piece(c), :]
        return remote(ref, ref, fold_sem.at[c], fold_got.at[c, 0], other)

    def slot(t):
        return slice(t * lanes, (t + 1) * lanes)

    def adjacent(t, sending):
        if t == 1:
            return mp < n_mp - 1 if sending else mp > 0
        return mp > 0 if sending else mp < n_mp - 1

    def near_far(t, sending, near, far):
        if 1 < t < n_mp - 1:
            far()
        else:
            pl.when(adjacent(t, sending))(near)
            pl.when(jnp.logical_not(adjacent(t, sending)))(far)

    def wo_copy(t):
        to = mp_at(t)
        return remote(
            w_right.at[cols(to * relays + turn, part), :],
            wo_all.at[cols(turn, part), slot(t)],
            wo_sem.at[0, t - 1],
            wo_sem.at[1, t - 1],
            {"mp": to},
        )

    def wo_whole(t):
        to = mp_at(t)
        return remote(
            w_right.at[cols(to, block), :],
            wo_all.at[:, slot(t)],
            wo_sem.at[0, t - 1],
            wo_sem.at[1, t - 1],
            {"mp": to},
        )

    def relay_out(t, s):
        ref = wo_all.at[cols(turn, part), slot(t)]
        to = {"dp": dp - turn + turn_at(s)}
        return remote(ref, ref, relay_sem.at[0, t - 1], relay_sem.at[1, t - 1], to)

    def relay_in(t, s):
        ref = wo_all.at[cols(turn_at(relays - s), part), slot(t)]
        to = {"dp": dp - turn + turn_at(s)}
        return remote(ref, ref, relay_sem.at[0, t - 1], relay_sem.at[1, t - 1], to)

    def ctx_copy(t):
        return remote(
            ctx_all.at[:, slot(0)],
            ctx_all.at[:, slot(t)],
            ctx_sem.at[0],
            ctx_sem.at[1],
            {"mp": mp_at(t)},
        )

    def mix_copy(c, b, j):
        ref = mix.at[b, piece(c), :]
        return remote(ref, ref, mix_send.at[c], mix_recv.at[c, b], {"mp": targets[j]})

    def fwd_copy(c, b):
        ref = mix.at[b, piece(c), :]
        return remote(ref, ref, fwd_sent.at[c], fwd_sem.at[c, b], other)

    def hid_copy(c):
        return remote(
            hid_own.at[piece(c), :], hid_other.at[piece(c), :], hid_sem.at[0, c], hid_sem.at[1, c], other
        )

    def fold_copy(c, k):
        if hubs:
            into = 1 + (1 - hub) * k if k else 0
            to = hub * arrivals[k] + (1 - hub) * mate
        else:
            into, to = k, arrivals[k]
        return remote(
            fold_send.at[k, piece(c), :],
            fold_recv.at[into, piece(c), :],
            fold_sem.at[c],
            fold_got.at[c, into],
            {"mp": to},
        )

    def fold_in(c, k):
        return remote(
            fold_send.at[0, piece(c), :],
            fold_recv.at[k, piece(c), :],
            fold_sem.at[c],
            fold_got.at[c, k],
            {"mp": arrivals[0]},
        )

    def send_own(c):
        for j in range(len(targets)):
            mix_copy(c, mp, j).start()

    kv_copy = remote(kv_send, kv_recv, kv_sem.at[0], kv_sem.at[1], other)
    gkv_copy = remote(g_send, g_all.at[0], gkv_sem.at[0], gkv_sem.at[1], other)
    down_copy = remote(
        ffn_out_hbm.at[:, cols(1 - sec, width // 2)], down_other, down_sem.at[0], down_sem.at[1], other
    )

    order = list(range(2, n_mp - 1)) + [1, n_mp - 1, 0]
    if n_dp == 4:
        beside = 1 + 2 * lax.rem(dp, 2)
        near_dp, far_dp = [beside, 2], [4 - beside]
    else:
        near_dp, far_dp = [1], list(range(2, n_dp))
    with jax.named_scope("signals"):
        barrier = pltpu.get_barrier_semaphore()
        for t in order:
            weight_load(t).start()
        for load in loads[:1]:
            load.start()
        signal(other)
        for t in range(1, n_dp):
            signal({"dp": dp_at(t)})
        for t in range(1, n_mp):
            signal({"mp": mp_at(t)})

    tile = 2 * lanes
    out_id = lax.broadcasted_iota(jnp.int32, (tile, tile), 0)
    in_id = lax.broadcasted_iota(jnp.int32, (tile, tile), 1)
    wanted = jnp.where(out_id < lanes, 2 * out_id, 2 * (out_id - lanes) + 1)
    pick = jnp.where(in_id == wanted, 1.0, 0.0).astype(BF16)
    first = lax.broadcasted_iota(jnp.int32, (lanes, lanes), 1) < half

    for t in order:
        with jax.named_scope("split%d" % t):
            begin = mp_at(t) * block
            weight_load(t).wait()
            for i in range(block // lanes):
                d = pl.multiple_of(begin + i * lanes, lanes)
                two = contract(pick, weight[pl.ds(pl.multiple_of(2 * d, tile), tile), :], 1, 0)
                one, second = two[:lanes], two[lanes:]
                w_left[pl.ds(d, lanes), :] = jnp.where(
                    first, one, pltpu.roll(second, half, 1)
                ).astype(BF16)
                w_right[pl.ds(d, lanes), :] = jnp.where(
                    first, pltpu.roll(one, half, 1), second
                ).astype(BF16)
        if t == order[0]:
            for load in loads[1:6]:
                load.start()
            with jax.named_scope("barrier"):
                pl.semaphore_wait(barrier, n_dp + n_mp - 1)

            @pl.when(is_enc)
            def _():
                for t in near_dp:
                    rows_copy(t).start()

        if t > 0:

            @pl.when(is_dec)
            def _():
                near_far(t, True, lambda: None, lambda: wo_copy(t).start())

    loads[0].wait()

    @pl.when(is_enc)
    def _():
        with jax.named_scope("kv"):
            kv_send[0] = contract(rows[...], w_left[...], 1, 0).astype(BF16)
            kv_send[1] = contract(rows[...], w_right[...], 1, 0).astype(BF16)
            kv_copy.start()

    for load in loads[6:]:
        load.start()
    own_rows.start()
    down_copy.start()
    for load in loads[1:6]:
        load.wait()

    @pl.when(is_dec)
    def _():
        own_grad.start()
        for t in (1, n_mp - 1):
            near_far(t, True, lambda: wo_whole(t).start(), lambda: None)
        with jax.named_scope("q_gc"):
            wide_q = contract(rows[...], w_left[...], 1, 0)
            wide_gc = contract(grad[...], w_right[...], 1, 0)
            q = wide_q.astype(BF16)
            gc = wide_gc.astype(BF16)
            dec = jnp.transpose(jnp.broadcast_to(dec_seg[...].astype(F32), (n_rows, n_rows)))
            same = dec == jnp.broadcast_to(enc_seg[...].astype(F32), (n_rows, n_rows))
            wo_all[:, slot(0)] = w_right[cols(mp, block), :]
        with jax.named_scope("kv_wait"):
            kv_copy.wait_recv()
        with jax.named_scope("attend"):
            key = kv_recv[0]
            value = kv_recv[1]
            probs, lows, contexts = [], [], []
            for h in range(2):
                mine = first if h == 0 else jnp.logical_not(first)
                scores = contract(jnp.where(mine, wide_q, 0.0).astype(BF16), key, 1, 1)
                scores = jnp.where(same, scores, -1e30)
                scores = jnp.exp(scores - jnp.max(scores, axis=1, keepdims=True))
                prob = scores / jnp.sum(scores, axis=1, keepdims=True)
                low = prob.astype(BF16)
                probs.append(prob)
                lows.append(low)
                contexts.append(contract(low, value, 1, 0))
            context = jnp.where(first, contexts[0], contexts[1]).astype(BF16)
            ctx_all[:, slot(0)] = context
            g_all[0, :, lanes:] = context
            for t in range(1, n_mp):
                ctx_copy(t).start()
        with jax.named_scope("relay"):
            for t in order[:-1]:

                def pass_quarter():
                    wo_copy(t).wait_recv()
                    for s in far_dp + near_dp if n_dp == relays else range(1, relays):
                        relay_out(t, s).start()

                near_far(t, False, lambda: None, pass_quarter)
        with jax.named_scope("attend_back"):
            gqs, gks, gvs = [], [], []
            for h in range(2):
                mine = first if h == 0 else jnp.logical_not(first)
                grad_prob = contract(jnp.where(mine, wide_gc, 0.0).astype(BF16), value, 1, 1)
                total = jnp.sum(grad_prob * probs[h], axis=1, keepdims=True)
                score = (probs[h] * (grad_prob - total)).astype(BF16)
                gqs.append(contract(score, key, 1, 0))
                gks.append(contract(score, q, 0, 0))
                gvs.append(contract(lows[h], gc, 0, 0))
            g_send[:, :lanes] = jnp.where(first, gks[0], gks[1]).astype(BF16)
            g_send[:, lanes:] = jnp.where(first, gvs[0], gvs[1]).astype(BF16)
            gkv_copy.start()
            g_all[0, :, :lanes] = jnp.where(first, gqs[0], gqs[1]).astype(BF16)

    @pl.when(is_enc)
    def _():
        with jax.named_scope("gkv_wait"):
            gkv_copy.wait_recv()
            for t in far_dp:
                rows_copy(t).start()

    @pl.when(is_dec)
    def _():
        with jax.named_scope("wo_wait"):
            for t in range(1, n_mp):

                def take_quarters():
                    if relays > 1:
                        relay_total(t).wait_recv()

                near_far(t, False, lambda: wo_whole(t).wait_recv(), take_quarters)
        for t in range(1, n_dp):
            rows_copy(t).start()
            grad_copy(t).start()
            g_copy(t).start()
        with jax.named_scope("ctx_wait"):
            ctx_total.wait_recv()
        with jax.named_scope("mix"):
            for c in range(pieces):
                own = contract(ctx_all[piece(c), :], wo_all[...], 1, 1)
                total = rows[piece(c), cols(mp, block)].astype(F32) + own
                mix[mp, piece(c), :] = total.astype(BF16)

                send_own(c)
                fwd_copy(c, mp).start()

    for load in loads[6:]:
        load.wait()

    def take(c, b, fresh):
        where = cols(b, block)
        wide = mix[b, piece(c), :].astype(F32)
        scaled = (wide * gain[:, where]).astype(BF16)
        both = contract(scaled, ffn_in[:, where], 1, 1)
        squares = jnp.sum(wide * wide, axis=1, keepdims=True)
        squares = jnp.broadcast_to(squares, (wide.shape[0], lanes))
        if fresh:
            gate_up[piece(c), :] = both
            square[piece(c), :] = squares
        else:
            gate_up[piece(c), :] += both
            square[piece(c), :] += squares

    place = sec * n_mp + mp
    def gather(c):
        @pl.when(is_enc)
        def _():
            fwd_copy(c, mp).wait_recv()
            if c == 0:
                for t in range(1, n_dp):
                    g_copy(t).start()

        take(c, mp, True)
        for k, b in enumerate(sequence):

            @pl.when(is_dec)
            def _():
                mix_copy(c, b, 0).wait_recv()
                fwd_copy(c, b).start()

            @pl.when(is_enc)
            def _():
                fwd_copy(c, b).wait_recv()

            take(c, b, False)

    def activate(c):
        with jax.named_scope("hidden%d" % c):
            inverse = lax.rsqrt(square[piece(c), :1] / width + norm_eps)
            gate = gate_up[piece(c), :units] * inverse
            up = gate_up[piece(c), units:] * inverse
            unit_level = level[...].astype(F32) * 0.25
            hidden = (jax.nn.gelu(gate, approximate=True) * up * unit_level).astype(BF16)
            hid_own[piece(c), :] = hidden
            hid_copy(c).start()

    def descend(c):
        with jax.named_scope("down_own%d" % c):
            hidden = hid_own[piece(c), :]
            for k in reversed(range(n_mp - 1)):
                partial[k, piece(c), :] = contract(hidden, down_own[:, cols(arrivals[k], share)], 1, 0)
        if c > 0:
            with jax.named_scope("combine%d" % (c - 1)):
                combine(c - 1)
        with jax.named_scope("hid_wait%d" % c):
            if c == 0:
                down_copy.wait_recv()
            hid_copy(c).wait_recv()
        with jax.named_scope("down%d" % c):
            beside_hidden = hid_other[piece(c), :]

            def product(b):
                where = cols(b, share)
                own = contract(hidden, down_own[:, where], 1, 0)
                return own + contract(beside_hidden, down_other[:, where], 1, 0)

            for k in reversed(range(n_mp - 1)):
                other_part = contract(beside_hidden, down_other[:, cols(arrivals[k], share)], 1, 0)
                own = partial[k, piece(c), :] + other_part
                fold_send[k, piece(c), :] = own.astype(BF16)
                if not hubs or k == 0:
                    fold_copy(c, k).start()
                else:
                    partial[k, piece(c), :] = own

                    @pl.when(jnp.logical_not(is_hub))
                    def _():
                        fold_copy(c, k).start()

            there = cols(lax.rem(place, 2), share)
            partial[0, piece(c), :] = product(mp) + mix[place // 2, piece(c), there].astype(F32)

    def combine(c):
        if hubs:

            @pl.when(is_hub)
            def _():
                for k in range(n_mp - 2, 0, -1):
                    fold_in(c, k + 1).wait_recv()
                    total = partial[k, piece(c), :] + fold_recv[k + 1, piece(c), :].astype(F32)
                    fold_send[k, piece(c), :] = total.astype(BF16)
                    fold_copy(c, k).start()

    for c in range(pieces):
        with jax.named_scope("gather%d" % c):
            gather(c)
        activate(c)
        descend(c)
    with jax.named_scope("combine%d" % (pieces - 1)):
        combine(pieces - 1)

    own_rows.wait()

    @pl.when(is_dec)
    def _():
        own_grad.wait()

    with jax.named_scope("dp_wait"):
        rows_total.wait_recv()
        g_total.wait_recv()

        @pl.when(is_dec)
        def _():
            grad_total.wait_recv()

    with jax.named_scope("weight_grads"):
        flat_rows = rows_all[...].reshape(n_dp * n_rows, cut)
        g_flat = g_all[...].reshape(n_dp * n_rows, 2 * lanes)
        t_left[...] = contract(g_flat[:, :lanes], flat_rows, 0, 0).astype(BF16)

        @pl.when(is_enc)
        def _():
            t_right[...] = contract(g_flat[:, lanes:], flat_rows, 0, 0).astype(BF16)

        @pl.when(is_dec)
        def _():
            flat_grad = grad_all[...].reshape(n_dp * n_rows, cut)
            t_right[...] = contract(g_flat[:, lanes:], flat_grad, 0, 0).astype(BF16)

        row_id = lax.broadcasted_iota(jnp.int32, (tile, lanes), 0)
        d_id = lax.broadcasted_iota(jnp.int32, (tile, lanes), 1)
        spread = [jnp.where(row_id == 2 * d_id + h, 1.0, 0.0).astype(BF16) for h in range(2)]
        for i in range(cut // lanes):
            some = slice(i * lanes, (i + 1) * lanes)
            heads = [
                jnp.concatenate(
                    [t_left[h * half : (h + 1) * half, some], t_right[h * half : (h + 1) * half, some]],
                    axis=0,
                )
                for h in range(2)
            ]
            woven = contract(spread[0], heads[0], 1, 1) + contract(spread[1], heads[1], 1, 1)
            proj_grads[i * tile : (i + 1) * tile, :] = woven.astype(BF16)

    with jax.named_scope("fold"):
        for c in range(pieces):
            mine = partial[0, piece(c), :]
            for k in range(2 if hubs else n_mp - 1):
                fold_in(c, k).wait_recv()
                mine = mine + fold_recv[k, piece(c), :].astype(F32)
            layer_out[piece(c), :] = mine.astype(BF16)

    with jax.named_scope("drain"):
        down_copy.wait_send()
        rows_total.wait_send()
        g_total.wait_send()
        for c in range(pieces):
            hid_copy(c).wait_send()
            fold_total(c).wait_send()

        @pl.when(is_enc)
        def _():
            kv_copy.wait_send()

        @pl.when(is_dec)
        def _():
            gkv_copy.wait_send()
            grad_total.wait_send()
            ctx_total.wait_send()
            for t in range(1, n_mp):
                near_far(t, True, lambda: wo_whole(t).wait_send(), lambda: wo_copy(t).wait_send())
                if relays > 1:
                    near_far(t, False, lambda: None, lambda: relay_total(t).wait_send())
            for c in range(pieces):
                mix_total(c, n_mp, fwd_sent).wait_send()
                mix_total(c, n_mp - 1, mix_send).wait_send()


def hand_over(a, b, a_out, b_out, sem):
    copies = [pltpu.make_async_copy(a, a_out, sem.at[0]), pltpu.make_async_copy(b, b_out, sem.at[1])]
    for copy in copies:
        copy.start()
    for copy in copies:
        copy.wait()


def on_device(
    n_dp,
    n_mp,
    section_rows,
    proj_weights,
    out_grad,
    ffn_gain,
    ffn_in,
    ffn_out,
    grow_level,
    dec_seg,
    enc_seg,
):
    rows = section_rows[0]
    n_rows, width = rows.shape
    heads, lanes = proj_weights.shape[2:]
    weight = proj_weights.reshape(width * heads, lanes)
    units = ffn_out.shape[0]
    gates = jnp.transpose(ffn_in, (1, 2, 0)).reshape(2 * units, width)
    block, share, cut = width // n_mp, width // (2 * n_mp), width // n_dp
    relays = math.gcd(n_dp, most_relays)
    vmem = pl.BlockSpec(memory_space=pltpu.VMEM)

    def sems(*shape):
        return pltpu.SemaphoreType.DMA(shape)

    operands = (
        rows,
        weight,
        out_grad,
        ffn_gain[None],
        gates,
        ffn_out,
        grow_level[None],
        dec_seg,
        enc_seg,
    )
    layer_out, grads = pl.pallas_call(
        functools.partial(body, n_dp, n_mp),
        out_shape=(
            pltpu.VMEM((n_rows, share), BF16),
            pltpu.VMEM((cut * heads, lanes), BF16),
        ),
        in_specs=[pl.BlockSpec(memory_space=pltpu.MemorySpace.HBM)] * 9,
        out_specs=(vmem, vmem),
        scratch_shapes=[pltpu.VMEM(a.shape, a.dtype) for a in operands if a is not ffn_out]
        + [
            pltpu.VMEM((units, width // 2), BF16),
            pltpu.VMEM((units, width // 2), BF16),
            pltpu.VMEM((width, lanes), BF16),
            pltpu.VMEM((width, lanes), BF16),
            pltpu.VMEM((2, n_rows, lanes), BF16),
            pltpu.VMEM((2, n_rows, lanes), BF16),
            pltpu.VMEM((block, n_mp * lanes), BF16),
            pltpu.VMEM((n_rows, n_mp * lanes), BF16),
            pltpu.VMEM((n_dp, n_rows, cut), BF16),
            pltpu.VMEM((n_dp, n_rows, cut), BF16),
            pltpu.VMEM((n_rows, 2 * lanes), BF16),
            pltpu.VMEM((n_dp, n_rows, 2 * lanes), BF16),
            pltpu.VMEM((n_mp, n_rows, block), BF16),
            pltpu.VMEM((n_rows, 2 * units), F32),
            pltpu.VMEM((n_rows, lanes), F32),
            pltpu.VMEM((n_rows, units), BF16),
            pltpu.VMEM((n_rows, units), BF16),
            pltpu.VMEM((n_mp, n_rows, share), F32),
            pltpu.VMEM((n_mp, n_rows, share), BF16),
            pltpu.VMEM((n_mp, n_rows, share), BF16),
            pltpu.VMEM((lanes, cut), BF16),
            pltpu.VMEM((lanes, cut), BF16),
            sems(2),
            sems(2),
            sems(2),
            sems(2, n_mp - 1),
            sems(2, n_mp - 1),
            sems(2),
            sems(pieces),
            sems(pieces, n_mp),
            sems(pieces),
            sems(pieces, n_mp),
            sems(2, pieces),
            sems(pieces),
            sems(pieces, n_mp),
            sems(2),
            sems(2),
            sems(2),
            sems(n_mp),
            sems(8),
            sems(2),
        ],
        compiler_params=pltpu.CompilerParams(
            collective_id=0, has_side_effects=True, vmem_limit_bytes=58 << 20
        ),
    )(*operands)
    layer_out, grads = pl.pallas_call(
        hand_over,
        out_shape=(
            jax.ShapeDtypeStruct(layer_out.shape, BF16),
            jax.ShapeDtypeStruct(grads.shape, BF16),
        ),
        in_specs=[vmem] * 2,
        out_specs=(pl.BlockSpec(memory_space=pl.ANY),) * 2,
        scratch_shapes=[pltpu.SemaphoreType.DMA((2,))],
    )(*(pltpu.with_memory_space_constraint(a, pltpu.VMEM) for a in (layer_out, grads)))
    return (layer_out, grads.reshape(1, cut, heads, lanes))


def solution(mesh):
    in_specs = (
        P("sec", "dp", None),
        P("sec", None, "mp", None),
        P("dp", None),
        P(),
        P(None, None, ("sec", "mp")),
        P(("sec", "mp"), None),
        P(("sec", "mp")),
        P("dp", None),
        P("dp", None),
    )
    out_specs = (P("dp", ("sec", "mp")), P("sec", "dp", "mp", None))
    return jax.shard_map(
        functools.partial(on_device, mesh.shape["dp"], mesh.shape["mp"]),
        mesh=mesh,
        in_specs=in_specs,
        out_specs=out_specs,
        check_vma=False,
    )
```

```python
import functools
import math

import jax
import jax.numpy as jnp
from jax import lax
from jax.experimental import pallas as pl
from jax.experimental.pallas import tpu as pltpu
from jax.sharding import PartitionSpec as P

norm_eps = 1e-06
eighths = (4, 4)
pieces = len(eighths)
most_relays = 4
F32 = jnp.float32
BF16 = jnp.bfloat16


def contract(left, right, left_dim, right_dim):
    dims = (((left_dim,), (right_dim,)), ((), ()))
    return lax.dot_general(left, right, dims, preferred_element_type=F32)


def remote(src, dst, send, recv, device):
    return pltpu.make_async_remote_copy(
        src_ref=src,
        dst_ref=dst,
        send_sem=send,
        recv_sem=recv,
        device_id=device,
        device_id_type=pl.DeviceIdType.MESH,
    )


def body(
    n_dp,
    n_mp,
    rows_hbm,
    weight_hbm,
    grad_hbm,
    gain_hbm,
    ffn_in_hbm,
    ffn_out_hbm,
    level_hbm,
    dec_seg_hbm,
    enc_seg_hbm,
    layer_out,
    proj_grads,
    rows,
    weight,
    grad,
    gain,
    ffn_in,
    level,
    dec_seg,
    enc_seg,
    down_own,
    down_other,
    w_left,
    w_right,
    kv_send,
    kv_recv,
    wo_all,
    ctx_all,
    rows_all,
    grad_all,
    g_send,
    g_all,
    mix,
    gate_up,
    square,
    hid_own,
    hid_other,
    partial,
    fold_send,
    fold_recv,
    t_left,
    t_right,
    rows_sem,
    grad_sem,
    g_sem,
    wo_sem,
    relay_sem,
    ctx_sem,
    mix_send,
    mix_recv,
    fwd_sent,
    fwd_sem,
    hid_sem,
    fold_sem,
    fold_got,
    kv_sem,
    gkv_sem,
    down_sem,
    weight_sem,
    load_sem,
    slot_sem,
):
    sec = lax.axis_index("sec")
    dp = lax.axis_index("dp")
    mp = lax.axis_index("mp")
    n_rows, width = rows.shape
    lanes = weight.shape[1]
    half = lanes // 2
    block = width // n_mp
    share = width // (2 * n_mp)
    cut = width // n_dp
    units = down_own.shape[0]
    hubs = n_mp == 4
    if hubs:
        hub = mp * (3 - mp) // 2
        mate = mp + 1 - 2 * lax.rem(mp, 2)
        far_hub = 3 - mp * hub - mate * (1 - hub)
        far_end = 3 - mate * hub - mp * (1 - hub)
        is_hub = hub == 1
    if hubs:
        arrivals = [mate, far_hub, far_end]
    else:
        arrivals = [lax.rem(mp + n_mp - t, n_mp) for t in range(1, n_mp)]
    if n_mp == 4:
        targets = [far_end, mate, far_hub]
        sequence = [mate, far_end, far_hub]
    else:
        targets = [lax.rem(mp + t, n_mp) for t in range(1, n_mp)]
        sequence = [lax.rem(mp + n_mp - t, n_mp) for t in range(1, n_mp)]
    starts = [sum(eighths[:c]) * n_rows // 8 for c in range(pieces + 1)]
    relays = math.gcd(n_dp, most_relays)
    part = block // relays
    turn = lax.rem(dp, relays)
    is_dec = sec == 1
    is_enc = sec == 0
    other = {"sec": 1 - sec}

    def dp_at(t):
        return lax.rem(dp + t, n_dp)

    def mp_at(t):
        return lax.rem(mp + t, n_mp)

    def turn_at(s):
        return lax.rem(turn + s, relays)

    def cols(index, size):
        return pl.ds(pl.multiple_of(index * size, size), size)

    def piece(c):
        return pl.ds(starts[c], starts[c + 1] - starts[c])

    def signal(device):
        pl.semaphore_signal(barrier, inc=1, device_id=device, device_id_type=pl.DeviceIdType.MESH)

    def weight_load(t):
        where = cols(mp_at(t), 2 * block)
        return pltpu.make_async_copy(
            weight_hbm.at[where, :], weight.at[where, :], weight_sem.at[t]
        )

    pairs = (
        (rows_hbm, rows),
        (grad_hbm, grad),
        (dec_seg_hbm, dec_seg),
        (enc_seg_hbm, enc_seg),
        (gain_hbm, gain),
        (level_hbm, level),
        (ffn_in_hbm, ffn_in),
        (ffn_out_hbm.at[:, cols(sec, width // 2)], down_own),
    )
    loads = [pltpu.make_async_copy(a, b, load_sem.at[i]) for i, (a, b) in enumerate(pairs)]
    own_rows = pltpu.make_async_copy(rows_hbm.at[:, cols(dp, cut)], rows_all.at[0], slot_sem.at[0])
    own_grad = pltpu.make_async_copy(grad_hbm.at[:, cols(dp, cut)], grad_all.at[0], slot_sem.at[1])

    def rows_copy(t):
        to = dp_at(t)
        return remote(
            rows_hbm.at[:, cols(to, cut)], rows_all.at[t], rows_sem.at[0], rows_sem.at[1], {"dp": to}
        )

    def grad_copy(t):
        to = dp_at(t)
        return remote(
            grad_hbm.at[:, cols(to, cut)], grad_all.at[t], grad_sem.at[0], grad_sem.at[1], {"dp": to}
        )

    def g_copy(t):
        return remote(
            g_all.at[0], g_all.at[t], g_sem.at[0], g_sem.at[1], {"dp": dp_at(t)}
        )

    def whole_of(ref, sem):
        return remote(ref, ref, sem.at[0], sem.at[1], other)

    peers = pl.ds(1, n_dp - 1)
    rows_total = whole_of(rows_all.at[peers], rows_sem)
    grad_total = whole_of(grad_all.at[peers], grad_sem)
    g_total = whole_of(g_all.at[peers], g_sem)
    ctx_total = whole_of(ctx_all.at[:, lanes:], ctx_sem)

    def relay_total(t):
        ref = wo_all.at[pl.ds(0, (relays - 1) * part), slot(t)]
        return remote(ref, ref, relay_sem.at[0, t - 1], relay_sem.at[1, t - 1], other)

    def mix_total(c, count, sem):
        ref = mix.at[pl.ds(0, count), piece(c), :]
        return remote(ref, ref, sem.at[c], mix_recv.at[c, 0], other)

    def fold_total(c):
        ref = fold_send.at[pl.ds(0, n_mp - 1), piece(c), :]
        return remote(ref, ref, fold_sem.at[c], fold_got.at[c, 0], other)

    def slot(t):
        return slice(t * lanes, (t + 1) * lanes)

    def adjacent(t, sending):
        if t == 1:
            return mp < n_mp - 1 if sending else mp > 0
        return mp > 0 if sending else mp < n_mp - 1

    def near_far(t, sending, near, far):
        if 1 < t < n_mp - 1:
            far()
        else:
            pl.when(adjacent(t, sending))(near)
            pl.when(jnp.logical_not(adjacent(t, sending)))(far)

    def wo_copy(t):
        to = mp_at(t)
        return remote(
            w_right.at[cols(to * relays + turn, part), :],
            wo_all.at[cols(turn, part), slot(t)],
            wo_sem.at[0, t - 1],
            wo_sem.at[1, t - 1],
            {"mp": to},
        )

    def wo_whole(t):
        to = mp_at(t)
        return remote(
            w_right.at[cols(to, block), :],
            wo_all.at[:, slot(t)],
            wo_sem.at[0, t - 1],
            wo_sem.at[1, t - 1],
            {"mp": to},
        )

    def relay_out(t, s):
        ref = wo_all.at[cols(turn, part), slot(t)]
        to = {"dp": dp - turn + turn_at(s)}
        return remote(ref, ref, relay_sem.at[0, t - 1], relay_sem.at[1, t - 1], to)

    def relay_in(t, s):
        ref = wo_all.at[cols(turn_at(relays - s), part), slot(t)]
        to = {"dp": dp - turn + turn_at(s)}
        return remote(ref, ref, relay_sem.at[0, t - 1], relay_sem.at[1, t - 1], to)

    def ctx_copy(t):
        return remote(
            ctx_all.at[:, slot(0)],
            ctx_all.at[:, slot(t)],
            ctx_sem.at[0],
            ctx_sem.at[1],
            {"mp": mp_at(t)},
        )

    def mix_copy(c, b, j):
        ref = mix.at[b, piece(c), :]
        return remote(ref, ref, mix_send.at[c], mix_recv.at[c, b], {"mp": targets[j]})

    def fwd_copy(c, b):
        ref = mix.at[b, piece(c), :]
        return remote(ref, ref, fwd_sent.at[c], fwd_sem.at[c, b], other)

    def hid_copy(c):
        return remote(
            hid_own.at[piece(c), :], hid_other.at[piece(c), :], hid_sem.at[0, c], hid_sem.at[1, c], other
        )

    def fold_copy(c, k):
        if hubs:
            into = 1 + (1 - hub) * k if k else 0
            to = hub * arrivals[k] + (1 - hub) * mate
        else:
            into, to = k, arrivals[k]
        return remote(
            fold_send.at[k, piece(c), :],
            fold_recv.at[into, piece(c), :],
            fold_sem.at[c],
            fold_got.at[c, into],
            {"mp": to},
        )

    def fold_in(c, k):
        return remote(
            fold_send.at[0, piece(c), :],
            fold_recv.at[k, piece(c), :],
            fold_sem.at[c],
            fold_got.at[c, k],
            {"mp": arrivals[0]},
        )

    def send_own(c):
        for j in range(len(targets)):
            mix_copy(c, mp, j).start()

    kv_copy = remote(kv_send, kv_recv, kv_sem.at[0], kv_sem.at[1], other)
    gkv_copy = remote(g_send, g_all.at[0], gkv_sem.at[0], gkv_sem.at[1], other)
    down_copy = remote(
        ffn_out_hbm.at[:, cols(1 - sec, width // 2)], down_other, down_sem.at[0], down_sem.at[1], other
    )

    order = list(range(2, n_mp - 1)) + [1, n_mp - 1, 0]
    if n_dp == 4:
        beside = 1 + 2 * lax.rem(dp, 2)
        near_dp, far_dp = [beside, 2], [4 - beside]
    else:
        near_dp, far_dp = [1], list(range(2, n_dp))
    with jax.named_scope("signals"):
        barrier = pltpu.get_barrier_semaphore()
        for t in order:
            weight_load(t).start()
        for load in loads[:1]:
            load.start()
        signal(other)
        for t in range(1, n_dp):
            signal({"dp": dp_at(t)})
        for t in range(1, n_mp):
            signal({"mp": mp_at(t)})

    tile = 2 * lanes
    out_id = lax.broadcasted_iota(jnp.int32, (tile, tile), 0)
    in_id = lax.broadcasted_iota(jnp.int32, (tile, tile), 1)
    wanted = jnp.where(out_id < lanes, 2 * out_id, 2 * (out_id - lanes) + 1)
    pick = jnp.where(in_id == wanted, 1.0, 0.0).astype(BF16)
    first = lax.broadcasted_iota(jnp.int32, (lanes, lanes), 1) < half

    for t in order:
        with jax.named_scope("split%d" % t):
            begin = mp_at(t) * block
            weight_load(t).wait()
            for i in range(block // lanes):
                d = pl.multiple_of(begin + i * lanes, lanes)
                two = contract(pick, weight[pl.ds(pl.multiple_of(2 * d, tile), tile), :], 1, 0)
                one, second = two[:lanes], two[lanes:]
                w_left[pl.ds(d, lanes), :] = jnp.where(
                    first, one, pltpu.roll(second, half, 1)
                ).astype(BF16)
                w_right[pl.ds(d, lanes), :] = jnp.where(
                    first, pltpu.roll(one, half, 1), second
                ).astype(BF16)
        if t == order[0]:
            for load in loads[1:6]:
                load.start()
            with jax.named_scope("barrier"):
                pl.semaphore_wait(barrier, n_dp + n_mp - 1)

            @pl.when(is_enc)
            def _():
                for t in near_dp:
                    rows_copy(t).start()

        if t > 0:

            @pl.when(is_dec)
            def _():
                near_far(t, True, lambda: None, lambda: wo_copy(t).start())

    loads[0].wait()

    @pl.when(is_enc)
    def _():
        with jax.named_scope("kv"):
            kv_send[0] = contract(rows[...], w_left[...], 1, 0).astype(BF16)
            kv_send[1] = contract(rows[...], w_right[...], 1, 0).astype(BF16)
            kv_copy.start()

    for load in loads[6:]:
        load.start()
    own_rows.start()
    down_copy.start()
    for load in loads[1:6]:
        load.wait()

    @pl.when(is_dec)
    def _():
        own_grad.start()
        for t in (1, n_mp - 1):
            near_far(t, True, lambda: wo_whole(t).start(), lambda: None)
        with jax.named_scope("q_gc"):
            wide_q = contract(rows[...], w_left[...], 1, 0)
            wide_gc = contract(grad[...], w_right[...], 1, 0)
            q = wide_q.astype(BF16)
            gc = wide_gc.astype(BF16)
            dec = jnp.transpose(jnp.broadcast_to(dec_seg[...].astype(F32), (n_rows, n_rows)))
            same = dec == jnp.broadcast_to(enc_seg[...].astype(F32), (n_rows, n_rows))
            wo_all[:, slot(0)] = w_right[cols(mp, block), :]
        with jax.named_scope("kv_wait"):
            kv_copy.wait_recv()
        with jax.named_scope("attend"):
            key = kv_recv[0]
            value = kv_recv[1]
            probs, lows, contexts = [], [], []
            for h in range(2):
                mine = first if h == 0 else jnp.logical_not(first)
                scores = contract(jnp.where(mine, wide_q, 0.0).astype(BF16), key, 1, 1)
                scores = jnp.where(same, scores, -1e30)
                scores = jnp.exp(scores - jnp.max(scores, axis=1, keepdims=True))
                prob = scores / jnp.sum(scores, axis=1, keepdims=True)
                low = prob.astype(BF16)
                probs.append(prob)
                lows.append(low)
                contexts.append(contract(low, value, 1, 0))
            context = jnp.where(first, contexts[0], contexts[1]).astype(BF16)
            ctx_all[:, slot(0)] = context
            g_all[0, :, lanes:] = context
            for t in range(1, n_mp):
                ctx_copy(t).start()
        with jax.named_scope("relay"):
            for t in order[:-1]:

                def pass_quarter():
                    wo_copy(t).wait_recv()
                    for s in far_dp + near_dp if n_dp == relays else range(1, relays):
                        relay_out(t, s).start()

                near_far(t, False, lambda: None, pass_quarter)
        with jax.named_scope("attend_back"):
            gqs, gks, gvs = [], [], []
            for h in range(2):
                mine = first if h == 0 else jnp.logical_not(first)
                grad_prob = contract(jnp.where(mine, wide_gc, 0.0).astype(BF16), value, 1, 1)
                total = jnp.sum(grad_prob * probs[h], axis=1, keepdims=True)
                score = (probs[h] * (grad_prob - total)).astype(BF16)
                gqs.append(contract(score, key, 1, 0))
                gks.append(contract(score, q, 0, 0))
                gvs.append(contract(lows[h], gc, 0, 0))
            g_send[:, :lanes] = jnp.where(first, gks[0], gks[1]).astype(BF16)
            g_send[:, lanes:] = jnp.where(first, gvs[0], gvs[1]).astype(BF16)
            gkv_copy.start()
            g_all[0, :, :lanes] = jnp.where(first, gqs[0], gqs[1]).astype(BF16)

    @pl.when(is_enc)
    def _():
        with jax.named_scope("gkv_wait"):
            gkv_copy.wait_recv()
            for t in far_dp:
                rows_copy(t).start()

    @pl.when(is_dec)
    def _():
        with jax.named_scope("wo_wait"):
            for t in range(1, n_mp):

                def take_quarters():
                    if relays > 1:
                        relay_total(t).wait_recv()

                near_far(t, False, lambda: wo_whole(t).wait_recv(), take_quarters)
        for t in range(1, n_dp):
            rows_copy(t).start()
            grad_copy(t).start()
            g_copy(t).start()
        with jax.named_scope("ctx_wait"):
            ctx_total.wait_recv()
        with jax.named_scope("mix"):
            for c in range(pieces):
                own = contract(ctx_all[piece(c), :], wo_all[...], 1, 1)
                total = rows[piece(c), cols(mp, block)].astype(F32) + own
                mix[mp, piece(c), :] = total.astype(BF16)

                send_own(c)
                fwd_copy(c, mp).start()

    for load in loads[6:]:
        load.wait()

    def take(c, b, fresh):
        where = cols(b, block)
        wide = mix[b, piece(c), :].astype(F32)
        scaled = (wide * gain[:, where]).astype(BF16)
        both = contract(scaled, ffn_in[:, where], 1, 1)
        squares = jnp.sum(wide * wide, axis=1, keepdims=True)
        squares = jnp.broadcast_to(squares, (wide.shape[0], lanes))
        if fresh:
            gate_up[piece(c), :] = both
            square[piece(c), :] = squares
        else:
            gate_up[piece(c), :] += both
            square[piece(c), :] += squares

    place = sec * n_mp + mp
    def gather(c):
        @pl.when(is_enc)
        def _():
            fwd_copy(c, mp).wait_recv()
            if c == 0:
                for t in range(1, n_dp):
                    g_copy(t).start()

        take(c, mp, True)
        for k, b in enumerate(sequence):

            @pl.when(is_dec)
            def _():
                mix_copy(c, b, 0).wait_recv()
                fwd_copy(c, b).start()

            @pl.when(is_enc)
            def _():
                fwd_copy(c, b).wait_recv()

            take(c, b, False)

    def activate(c):
        with jax.named_scope("hidden%d" % c):
            inverse = lax.rsqrt(square[piece(c), :1] / width + norm_eps)
            gate = gate_up[piece(c), :units] * inverse
            up = gate_up[piece(c), units:] * inverse
            unit_level = level[...].astype(F32) * 0.25
            hidden = (jax.nn.gelu(gate, approximate=True) * up * unit_level).astype(BF16)
            hid_own[piece(c), :] = hidden
            hid_copy(c).start()

    def descend(c):
        with jax.named_scope("down_own%d" % c):
            hidden = hid_own[piece(c), :]
            for k in reversed(range(n_mp - 1)):
                partial[k, piece(c), :] = contract(hidden, down_own[:, cols(arrivals[k], share)], 1, 0)
        if c > 0:
            with jax.named_scope("combine%d" % (c - 1)):
                combine(c - 1)
        with jax.named_scope("hid_wait%d" % c):
            if c == 0:
                down_copy.wait_recv()
            hid_copy(c).wait_recv()
        with jax.named_scope("down%d" % c):
            beside_hidden = hid_other[piece(c), :]

            def product(b):
                where = cols(b, share)
                own = contract(hidden, down_own[:, where], 1, 0)
                return own + contract(beside_hidden, down_other[:, where], 1, 0)

            for k in reversed(range(n_mp - 1)):
                other_part = contract(beside_hidden, down_other[:, cols(arrivals[k], share)], 1, 0)
                own = partial[k, piece(c), :] + other_part
                fold_send[k, piece(c), :] = own.astype(BF16)
                if not hubs or k == 0:
                    fold_copy(c, k).start()
                else:
                    partial[k, piece(c), :] = own

                    @pl.when(jnp.logical_not(is_hub))
                    def _():
                        fold_copy(c, k).start()

            there = cols(lax.rem(place, 2), share)
            partial[0, piece(c), :] = product(mp) + mix[place // 2, piece(c), there].astype(F32)

    def combine(c):
        if hubs:

            @pl.when(is_hub)
            def _():
                for k in range(n_mp - 2, 0, -1):
                    fold_in(c, k + 1).wait_recv()
                    total = partial[k, piece(c), :] + fold_recv[k + 1, piece(c), :].astype(F32)
                    fold_send[k, piece(c), :] = total.astype(BF16)
                    fold_copy(c, k).start()

    for c in range(pieces):
        with jax.named_scope("gather%d" % c):
            gather(c)
        activate(c)
        descend(c)
    with jax.named_scope("combine%d" % (pieces - 1)):
        combine(pieces - 1)

    own_rows.wait()

    @pl.when(is_dec)
    def _():
        own_grad.wait()

    with jax.named_scope("dp_wait"):
        rows_total.wait_recv()
        g_total.wait_recv()

        @pl.when(is_dec)
        def _():
            grad_total.wait_recv()

    with jax.named_scope("weight_grads"):
        flat_rows = rows_all[...].reshape(n_dp * n_rows, cut)
        g_flat = g_all[...].reshape(n_dp * n_rows, 2 * lanes)
        t_left[...] = contract(g_flat[:, :lanes], flat_rows, 0, 0).astype(BF16)

        @pl.when(is_enc)
        def _():
            t_right[...] = contract(g_flat[:, lanes:], flat_rows, 0, 0).astype(BF16)

        @pl.when(is_dec)
        def _():
            flat_grad = grad_all[...].reshape(n_dp * n_rows, cut)
            t_right[...] = contract(g_flat[:, lanes:], flat_grad, 0, 0).astype(BF16)

        row_id = lax.broadcasted_iota(jnp.int32, (tile, lanes), 0)
        d_id = lax.broadcasted_iota(jnp.int32, (tile, lanes), 1)
        spread = [jnp.where(row_id == 2 * d_id + h, 1.0, 0.0).astype(BF16) for h in range(2)]
        for i in range(cut // lanes):
            some = slice(i * lanes, (i + 1) * lanes)
            heads = [
                jnp.concatenate(
                    [t_left[h * half : (h + 1) * half, some], t_right[h * half : (h + 1) * half, some]],
                    axis=0,
                )
                for h in range(2)
            ]
            woven = contract(spread[0], heads[0], 1, 1) + contract(spread[1], heads[1], 1, 1)
            proj_grads[i * tile : (i + 1) * tile, :] = woven.astype(BF16)

    with jax.named_scope("fold"):
        for c in range(pieces):
            mine = partial[0, piece(c), :]
            for k in range(2 if hubs else n_mp - 1):
                fold_in(c, k).wait_recv()
                mine = mine + fold_recv[k, piece(c), :].astype(F32)
            layer_out[piece(c), :] = mine.astype(BF16)

    with jax.named_scope("drain"):
        down_copy.wait_send()
        rows_total.wait_send()
        g_total.wait_send()
        for c in range(pieces):
            hid_copy(c).wait_send()
            fold_total(c).wait_send()

        @pl.when(is_enc)
        def _():
            kv_copy.wait_send()

        @pl.when(is_dec)
        def _():
            gkv_copy.wait_send()
            grad_total.wait_send()
            ctx_total.wait_send()
            for t in range(1, n_mp):
                near_far(t, True, lambda: wo_whole(t).wait_send(), lambda: wo_copy(t).wait_send())
                if relays > 1:
                    near_far(t, False, lambda: None, lambda: relay_total(t).wait_send())
            for c in range(pieces):
                mix_total(c, n_mp, fwd_sent).wait_send()
                mix_total(c, n_mp - 1, mix_send).wait_send()


def hand_over(a, b, a_out, b_out, sem):
    copies = [pltpu.make_async_copy(a, a_out, sem.at[0]), pltpu.make_async_copy(b, b_out, sem.at[1])]
    for copy in copies:
        copy.start()
    for copy in copies:
        copy.wait()


def on_device(
    n_dp,
    n_mp,
    section_rows,
    proj_weights,
    out_grad,
    ffn_gain,
    ffn_in,
    ffn_out,
    grow_level,
    dec_seg,
    enc_seg,
):
    rows = section_rows[0]
    n_rows, width = rows.shape
    heads, lanes = proj_weights.shape[2:]
    weight = proj_weights.reshape(width * heads, lanes)
    units = ffn_out.shape[0]
    gates = jnp.transpose(ffn_in, (1, 2, 0)).reshape(2 * units, width)
    block, share, cut = width // n_mp, width // (2 * n_mp), width // n_dp
    relays = math.gcd(n_dp, most_relays)
    vmem = pl.BlockSpec(memory_space=pltpu.VMEM)

    def sems(*shape):
        return pltpu.SemaphoreType.DMA(shape)

    operands = (
        rows,
        weight,
        out_grad,
        ffn_gain[None],
        gates,
        ffn_out,
        grow_level[None],
        dec_seg,
        enc_seg,
    )
    layer_out, grads = pl.pallas_call(
        functools.partial(body, n_dp, n_mp),
        out_shape=(
            pltpu.VMEM((n_rows, share), BF16),
            pltpu.VMEM((cut * heads, lanes), BF16),
        ),
        in_specs=[pl.BlockSpec(memory_space=pltpu.MemorySpace.HBM)] * 9,
        out_specs=(vmem, vmem),
        scratch_shapes=[pltpu.VMEM(a.shape, a.dtype) for a in operands if a is not ffn_out]
        + [
            pltpu.VMEM((units, width // 2), BF16),
            pltpu.VMEM((units, width // 2), BF16),
            pltpu.VMEM((width, lanes), BF16),
            pltpu.VMEM((width, lanes), BF16),
            pltpu.VMEM((2, n_rows, lanes), BF16),
            pltpu.VMEM((2, n_rows, lanes), BF16),
            pltpu.VMEM((block, n_mp * lanes), BF16),
            pltpu.VMEM((n_rows, n_mp * lanes), BF16),
            pltpu.VMEM((n_dp, n_rows, cut), BF16),
            pltpu.VMEM((n_dp, n_rows, cut), BF16),
            pltpu.VMEM((n_rows, 2 * lanes), BF16),
            pltpu.VMEM((n_dp, n_rows, 2 * lanes), BF16),
            pltpu.VMEM((n_mp, n_rows, block), BF16),
            pltpu.VMEM((n_rows, 2 * units), F32),
            pltpu.VMEM((n_rows, lanes), F32),
            pltpu.VMEM((n_rows, units), BF16),
            pltpu.VMEM((n_rows, units), BF16),
            pltpu.VMEM((n_mp, n_rows, share), F32),
            pltpu.VMEM((n_mp, n_rows, share), BF16),
            pltpu.VMEM((n_mp, n_rows, share), BF16),
            pltpu.VMEM((lanes, cut), BF16),
            pltpu.VMEM((lanes, cut), BF16),
            sems(2),
            sems(2),
            sems(2),
            sems(2, n_mp - 1),
            sems(2, n_mp - 1),
            sems(2),
            sems(pieces),
            sems(pieces, n_mp),
            sems(pieces),
            sems(pieces, n_mp),
            sems(2, pieces),
            sems(pieces),
            sems(pieces, n_mp),
            sems(2),
            sems(2),
            sems(2),
            sems(n_mp),
            sems(8),
            sems(2),
        ],
        compiler_params=pltpu.CompilerParams(
            collective_id=0, has_side_effects=True, vmem_limit_bytes=58 << 20
        ),
    )(*operands)
    layer_out, grads = pl.pallas_call(
        hand_over,
        out_shape=(
            jax.ShapeDtypeStruct(layer_out.shape, BF16),
            jax.ShapeDtypeStruct(grads.shape, BF16),
        ),
        in_specs=[vmem] * 2,
        out_specs=(pl.BlockSpec(memory_space=pl.ANY),) * 2,
        scratch_shapes=[pltpu.SemaphoreType.DMA((2,))],
    )(*(pltpu.with_memory_space_constraint(a, pltpu.VMEM) for a in (layer_out, grads)))
    return (layer_out, grads.reshape(1, cut, heads, lanes))


def solution(mesh):
    in_specs = (
        P("sec", "dp", None),
        P("sec", None, "mp", None),
        P("dp", None),
        P(),
        P(None, None, ("sec", "mp")),
        P(("sec", "mp"), None),
        P(("sec", "mp")),
        P("dp", None),
        P("dp", None),
    )
    out_specs = (P("dp", ("sec", "mp")), P("sec", "dp", "mp", None))
    return jax.shard_map(
        functools.partial(on_device, mesh.shape["dp"], mesh.shape["mp"]),
        mesh=mesh,
        in_specs=in_specs,
        out_specs=out_specs,
        check_vma=False,
    )
```
